128 devices in a mesh: row: 8 (over y, core), col: 16 (over x, z).
Axes of the slice: x: 4, y: 4, z: 4, core: 2. Of those that a mesh axis runs over, the one named last changes fastest.
Arguments:
- probes: bfloat16 [4, 32768, 256], P(None, ('row', 'col')), may hold values from -6 to 6
- points: bfloat16 [16, 4, 32768], P(None, None, ('row', 'col')), may hold values from -8 to 8
- leaf_skeleton: int32 [256, 64], P(('row', 'col')), may hold values from 0 to 127, as said below
- skeleton_one: int32 [128, 64], P(('row', 'col')), may hold values from 0 to 127, as said below
- skeleton_two: int32 [64, 64], P('row'), may hold values from 0 to 127, as said below
- skeleton_three: int32 [32, 64], P('row'), may hold values from 0 to 127, as said below
Outputs:
- leaf_interp: float32 [256, 128, 64], P(('row', 'col'))
- upper_interp: float32 [3, 128, 128, 64], P(None, ('row', 'col'))
- top_state: float32 [2, 128, 64, 256], P(None, ('row', 'col'))
The draws below stay inside these ranges and needn't reach their ends.
Inputs may be any that keep to these rules, and one draw needn't show every extreme that they name: `leaf_skeleton`: each row names 64 different rows of its leaf, in ascending order. `skeleton_one`: each row names 64 different rows of the node's stacked child skeletons, in ascending order. `skeleton_two`: each row names 64 different rows of the node's stacked child skeletons, in ascending order. `skeleton_three`: each row names 64 different rows of the node's stacked child skeletons, in ascending order.
All inputs are finite; a program needn't handle non-finite values.
Results may differ from the reference program's by a relative error of at most 0.0059.
Values may be sent and summed in bfloat16 or wider, within the bound.
A program may use at most 64 MiB of HBM per device.

```python
import math
import jax
import jax.numpy as jnp
from jax import lax

LEAF = 128
RANK = 64
SAMPLES = 256
FEAT = 16
N = 32768


def choose_rows(key, count, pool):
    scores = jax.random.randint(key, (count, pool), 0, 1 << 20) * pool + jnp.arange(pool, dtype=jnp.int32)[None, :]
    order = jnp.argsort(scores, axis=1)[:, :RANK]
    return jnp.sort(order, axis=1).astype(jnp.int32)


def draw_points(key, part):
    first_key, second_key = jax.random.split(jax.random.fold_in(key, 7), 2)
    total_nodes = 4 * N
    stride = 4 * LEAF
    coarse = 0.8 * jax.random.normal(first_key, (FEAT, total_nodes // stride + 1), jnp.float32)
    offsets = jnp.arange(total_nodes, dtype=jnp.int32)
    lower_index = offsets // stride
    fraction = (offsets % stride).astype(jnp.float32) / stride
    smooth = coarse[:, lower_index] * (1.0 - fraction) + coarse[:, lower_index + 1] * fraction
    rough_part = 1.6 * jax.random.normal(second_key, (FEAT, total_nodes), jnp.float32)
    return jnp.clip(smooth + rough_part, -8.0, 8.0).reshape(FEAT, 4, N).astype(jnp.bfloat16)


def draw_leaf_skeleton(key, part):
    return choose_rows(jax.random.fold_in(key, 11), N // LEAF, LEAF)


def draw_skeleton_one(key, part):
    return choose_rows(jax.random.fold_in(key, 13), N // (2 * LEAF), 2 * RANK)


def draw_skeleton_two(key, part):
    return choose_rows(jax.random.fold_in(key, 17), N // (4 * LEAF), 2 * RANK)


def draw_skeleton_three(key, part):
    return choose_rows(jax.random.fold_in(key, 19), N // (8 * LEAF), 2 * RANK)


def level_of(stream_key, dims, cuts, low, largest):
    loudness, own = 1.0, jax.random.fold_in(stream_key, 6)
    for dim, blocks in cuts:
        heights = jnp.exp(jax.random.uniform(jax.random.fold_in(own, dim), (blocks,), jnp.float32, low / len(cuts), largest / len(cuts)))
        loudness = loudness * jnp.repeat(heights, dims[dim] // blocks).reshape([-1 if axis == dim else 1 for axis in range(len(dims))])
    return loudness


def noise(own_key, shape, scale, most, shards=(), kind=jnp.bfloat16):
    array = jax.random.normal(own_key, shape, jnp.float32) * scale
    if len(shards) > 0:
        array = level_of(own_key, shape, shards, -0.22, 0.18) * array
    return jnp.clip(array, min=-most, max=most).astype(kind)


def setup_inputs(seed: int = 0) -> dict:
    arg_keys = jax.random.split(jax.random.key(seed), 7)
    return {
        "probes": noise(arg_keys[0], (4, N, SAMPLES), 1.0, 6.0, ((1, 128),)),
        "points": draw_points(jax.random.fold_in(arg_keys[6], 71), 0),
        "leaf_skeleton": draw_leaf_skeleton(jax.random.fold_in(arg_keys[6], 71), 0),
        "skeleton_one": draw_skeleton_one(jax.random.fold_in(arg_keys[6], 71), 0),
        "skeleton_two": draw_skeleton_two(jax.random.fold_in(arg_keys[6], 71), 0),
        "skeleton_three": draw_skeleton_three(jax.random.fold_in(arg_keys[6], 71), 0),
    }


exact_mode = lax.Precision.HIGHEST

def couple(row_feats, col_feats, kernel_gain):
    cross = jnp.dot(row_feats.T, col_feats, precision=exact_mode)
    row_sq = lax.optimization_barrier(jnp.sum(row_feats * row_feats, axis=0))
    col_sq = lax.optimization_barrier(jnp.sum(col_feats * col_feats, axis=0))
    feat_count = row_feats.shape[0]
    return kernel_gain * jnp.exp((2.0 * cross - row_sq[:, None] - col_sq[None, :]) / (2.0 * feat_count))

def interpolate(stacked, chosen):
    skeleton = jnp.take(stacked, chosen, axis=0)
    gram_mat = jnp.dot(skeleton, skeleton.T, precision=exact_mode)
    damping = 0.05 * jnp.sum(skeleton * skeleton) / chosen.shape[0] + 1e-05
    factor = jnp.linalg.cholesky(gram_mat + damping * jnp.eye(chosen.shape[0], dtype=stacked.dtype))
    cross_mat = jnp.dot(stacked, skeleton.T, precision=exact_mode)
    solved = jax.scipy.linalg.cho_solve((factor, True), cross_mat.T)
    return (solved.T, skeleton)

def leaf_level(leaf_rows, leaf_probes, coords, chosen):
    interp, skeleton = interpolate(leaf_rows, chosen)
    reduced = jnp.dot(interp.T, leaf_probes.astype(interp.dtype), precision=exact_mode)
    picked = jnp.take(coords, chosen, axis=1).astype(jnp.float32)
    return (interp, (skeleton, reduced, picked))

def merge_pair(first_child, second_child, chosen, kernel_gain):
    first_samples, first_reduced, first_points = first_child
    second_samples, second_reduced, second_points = second_child
    upper_rows = first_samples - jnp.dot(couple(first_points, second_points, kernel_gain), second_reduced, precision=exact_mode)
    lower_rows = second_samples - jnp.dot(couple(second_points, first_points, kernel_gain), first_reduced, precision=exact_mode)
    stacked = jnp.concatenate([upper_rows, lower_rows], axis=0)
    interp, skeleton = interpolate(stacked, chosen)
    reduced = jnp.dot(interp.T, jnp.concatenate([first_reduced, second_reduced], axis=0), precision=exact_mode)
    joined = jnp.take(jnp.concatenate([first_points, second_points], axis=1), chosen, axis=1)
    return (interp, (skeleton, reduced, joined))

def take_evens(values):
    return values[0::2]

def take_odds(values):
    return values[1::2]

def reference(probes, points, leaf_skeleton, skeleton_one, skeleton_two, skeleton_three):
    feat_count = points.shape[0]
    extent = points.shape[2]
    total = 4 * extent
    kernel_gain = 16.0 / math.sqrt(total)
    all_points = points.reshape(feat_count, total).astype(jnp.float32)
    all_probes = probes.reshape(total, -1)
    indices = jnp.arange(total, dtype=jnp.int32)
    probes_wide = all_probes.astype(jnp.float32)
    height = min(512, extent)

    def sample_block(start_row):
        coords = lax.dynamic_slice_in_dim(all_points, start_row, height, 1)
        row_ids = start_row + jnp.arange(height, dtype=jnp.int32)
        kernel_tile = couple(coords, all_points, kernel_gain)
        kernel_tile = jnp.where((row_ids // LEAF)[:, None] == (indices // LEAF)[None, :], 0.0, kernel_tile)
        kernel_tile = lax.optimization_barrier(kernel_tile.astype(jnp.bfloat16)).astype(jnp.float32)
        return jnp.dot(kernel_tile, probes_wide, precision=exact_mode)
    starts = jnp.arange(extent // height, dtype=jnp.int32) * height
    samples = lax.map(sample_block, starts).reshape(extent, -1)
    leaf_count = extent // LEAF
    leaf_rows = samples.reshape(leaf_count, LEAF, -1)
    leaf_probes = probes[0].reshape(leaf_count, LEAF, -1)
    leaf_coords = points[:, 0].reshape(feat_count, leaf_count, LEAF).transpose(1, 0, 2)
    leaf_interp, carried = jax.vmap(leaf_level)(leaf_rows, leaf_probes, leaf_coords, leaf_skeleton)
    upper_list = []
    for level_num, chosen in enumerate((skeleton_one, skeleton_two, skeleton_three)):
        first_child = jax.tree.map(take_evens, carried)
        second_child = jax.tree.map(take_odds, carried)
        interp, carried = jax.vmap(merge_pair, in_axes=(0, 0, 0, None))(first_child, second_child, chosen, kernel_gain)
        upper_list.append(jnp.repeat(interp, 2 ** level_num, axis=0))
    upper_interp = jnp.stack(upper_list)
    top_state = jnp.stack([jnp.repeat(carried[0], 4, axis=0), jnp.repeat(carried[1], 4, axis=0)])
    return (leaf_interp, upper_interp, top_state)
```

```python
from functools import partial
import math

import jax
import jax.numpy as jnp
from jax import lax
from jax.experimental import pallas as pl
from jax.experimental.pallas import tpu as pltpu
from jax.sharding import PartitionSpec as P

LEAF = 128
MESH = pl.DeviceIdType.MESH
exact_mode = lax.Precision.HIGHEST
LOG2E = math.log2(math.e)
SIDE = 4
OWN = 256
CHUNK = 4 * OWN
FEATS = 64
PLACE = {(0, 0): 0, (0, 1): 1, (1, 0): 2, (3, 0): 3, (1, 1): 4, (3, 1): 5, (2, 0): 6, (2, 1): 7}
EARLY = 3


def pieces(value):
    high = value.astype(jnp.bfloat16).astype(jnp.float32)
    rest = value - high
    mid = rest.astype(jnp.bfloat16).astype(jnp.float32)
    return high, mid, rest - mid


def extra_rows(first, second):
    row = lax.broadcasted_iota(jnp.int32, (16, OWN), 0)
    out = jnp.zeros((16, OWN), jnp.float32)
    for i, value in enumerate((*first, *second)):
        out = jnp.where(row == i, value, out)
    return out


def spread(i):
    return lax.rem(2 + i + lax.div(i * (i - 1), 2), SIDE)


def sample_kernel(gain, probes, points, out, prb, pts, rpts, colf, rowf, acc, outbox, inbox,
                  loc_sem, rp_send, rp_recv, chip_send, up_send, down_send, got, box_send, box_recv):
    row, col = lax.axis_index("row"), lax.axis_index("col")
    y, core = row // 2, lax.rem(row, 2)
    x, z = col // SIDE, lax.rem(col, SIDE)
    up = lax.rem(y + 1, SIDE) * 2 + core
    down = lax.rem(y + 3, SIDE) * 2 + core
    partner = y * 2 + 1 - core

    local = [pltpu.make_async_copy(probes.at[q], prb.at[pl.ds(q * OWN, OWN)], loc_sem.at[q]) for q in range(4)]
    local.append(pltpu.make_async_copy(points, pts.at[0], loc_sem.at[4]))
    local.append(pltpu.make_async_copy(points.at[0], rpts.at[0], loc_sem.at[5]))
    for copy in local:
        copy.start()

    def peer_col(j, sign):
        dx, dz = j // SIDE, lax.rem(j, SIDE)
        return lax.rem(x + sign * dx + SIDE, SIDE) * SIDE + lax.rem(z + sign * dz + SIDE, SIDE)

    barrier = pltpu.get_barrier_semaphore()
    for other in (up, down, partner):
        pl.semaphore_signal(barrier, inc=1, device_id=(other, col), device_id_type=MESH)

    def greet(j, _):
        pl.semaphore_signal(barrier, inc=1, device_id=(row, peer_col(j, 1)), device_id_type=MESH)
        return 0

    lax.fori_loop(1, 16, greet, 0)
    for copy in local:
        copy.wait()
    pl.semaphore_wait(barrier, 18)

    def row_copy(j):
        return pltpu.make_async_remote_copy(
            src_ref=rpts.at[0], dst_ref=rpts.at[j], send_sem=rp_send.at[j], recv_sem=rp_recv.at[j],
            device_id=(row, peer_col(j, 1)), device_id_type=MESH)

    def send_row(j, _):
        row_copy(j).start()
        return 0

    def piece_copy(src, dst, q, sem, target):
        src_ref = pts.at[src] if q == 4 else prb.at[pl.ds(src * CHUNK + q * OWN, OWN)]
        dst_ref = pts.at[dst] if q == 4 else prb.at[pl.ds(dst * CHUNK + q * OWN, OWN)]
        return pltpu.make_async_remote_copy(
            src_ref=src_ref, dst_ref=dst_ref, send_sem=sem, recv_sem=got.at[dst, q],
            device_id=(target, col), device_id_type=MESH)

    def on_chip(dy, q):
        return piece_copy(PLACE[dy, 0], PLACE[dy, 1], q, chip_send.at[dy, q], partner)

    def upward(src_dy, q):
        return piece_copy(PLACE[src_dy, 0], PLACE[src_dy + 1, 0], q, up_send.at[src_dy, q], up)

    def downward(src_dy, q):
        return piece_copy(PLACE[src_dy, 0], PLACE[3 if src_dy == 0 else 2, 0], q, down_send.at[src_dy // 3, q], down)

    def arrived(dy, dc, q):
        place = PLACE[dy, dc]
        piece_copy(place, place, q, chip_send.at[0, 0], partner).wait_recv()

    on_chip(0, 4).start()
    upward(0, 4).start()
    downward(0, 4).start()
    lax.fori_loop(1, 16, send_row, 0)
    for q in range(4):
        on_chip(0, q).start()
    for q, r in zip((0, 1, 2, 3), (2, 3, 0, 1)):
        upward(0, q).start()
        downward(0, r).start()

    def col_features(place):
        for q in range(4):
            feats = pts[place, q].astype(jnp.float32)
            bias = jnp.sum(feats * feats, axis=0, keepdims=True) * (-LOG2E / 32)
            ones = (jnp.float32(1),) * 3
            stacked = jnp.concatenate([feats, feats, feats, extra_rows(ones, pieces(bias))], axis=0)
            colf[:, pl.ds(place * CHUNK + q * OWN, OWN)] = stacked.astype(jnp.bfloat16)

    def row_features(j):
        feats = rpts[j].astype(jnp.float32)
        bias = math.log2(gain) - jnp.sum(feats * feats, axis=0, keepdims=True) * (LOG2E / 32)
        ones = (jnp.float32(1),) * 3
        stacked = jnp.concatenate([*pieces(feats * (LOG2E / 16)), extra_rows(pieces(bias), ones)], axis=0)
        rowf[pl.ds(pl.multiple_of(j * OWN, OWN), OWN), :] = stacked.T.astype(jnp.bfloat16)

    def block(j, first, last):
        rows = rowf[pl.ds(pl.multiple_of(j * OWN, OWN), OWN), :]
        cols = pl.ds(first * CHUNK, (last - first) * CHUNK)
        power = jnp.dot(rows, colf[:, cols], preferred_element_type=jnp.float32)
        return jnp.exp2(power).astype(jnp.bfloat16), prb[cols, :]

    def at(j):
        return pl.ds(pl.multiple_of(j * OWN, OWN), OWN)

    col_features(0)
    row_features(0)
    power = jnp.dot(rowf[pl.ds(0, OWN), :], colf[:, pl.ds(0, CHUNK)], preferred_element_type=jnp.float32)
    leaf_of = lax.broadcasted_iota(jnp.int32, (OWN, CHUNK), 0) // LEAF
    other_leaf = lax.broadcasted_iota(jnp.int32, (OWN, CHUNK), 1) // LEAF
    tile = jnp.where(leaf_of == other_leaf, 0.0, jnp.exp2(power)).astype(jnp.bfloat16)
    own_sum = jnp.dot(tile, prb[pl.ds(0, CHUNK), :], preferred_element_type=jnp.float32)
    for q in (4, 0, 1, 2, 3):
        arrived(0, 1, q)
    col_features(1)
    tile, rows = block(0, 1, 2)
    acc[pl.ds(0, OWN), :] = own_sum + jnp.dot(tile, rows, preferred_element_type=jnp.float32)

    def near_block(j, _):
        row_copy(j).wait_recv()
        row_features(j)
        tile, rows = block(j, 0, 2)
        acc[at(j), :] = jnp.dot(tile, rows, preferred_element_type=jnp.float32)

        @pl.when(j == 10)
        def _():
            for q in (4, 0, 1):
                arrived(1, 0, q)
                upward(1, q).start()
                on_chip(1, q).start()
            for q in (4, 2, 3):
                arrived(3, 0, q)
                if q != 4:
                    downward(3, q).start()
                on_chip(3, q).start()
        return 0

    lax.fori_loop(1, 16, near_block, 0)
    for q, r in ((2, 0), (3, 1)):
        arrived(1, 0, q)
        on_chip(1, q).start()
        arrived(3, 0, r)
        on_chip(3, r).start()
    for place in range(2, EARLY):
        col_features(place)

    def mid_block(j, _):
        tile, rows = block(j, 2, EARLY)
        acc[at(j), :] += jnp.dot(tile, rows, preferred_element_type=jnp.float32)

        @pl.when(j == 12)
        def _():
            for q in (4, 0, 2, 1, 3):
                arrived(2, 0, q)
                on_chip(2, q).start()
        return 0

    lax.fori_loop(0, 16, mid_block, 0)
    for dy in (1, 3, 2):
        for q in (4, 0, 1, 2, 3):
            arrived(dy, 1, q)
    for place in range(EARLY, 8):
        col_features(place)

    def box_copy(j):
        return pltpu.make_async_remote_copy(
            src_ref=outbox.at[j], dst_ref=inbox.at[j], send_sem=box_send.at[j], recv_sem=box_recv.at[j],
            device_id=(row, peer_col(j, -1)), device_id_type=MESH)

    def last_block(i, _):
        j = spread(i // SIDE) * SIDE + spread(lax.rem(i, SIDE))
        tile, rows = block(j, EARLY, 8)
        total = acc[at(j), :] + jnp.dot(tile, rows, preferred_element_type=jnp.float32)
        outbox[j] = total.astype(jnp.bfloat16)
        box_copy(j).start()
        return 0

    lax.fori_loop(0, 15, last_block, 0)
    tile, rows = block(0, EARLY, 8)
    acc[pl.ds(0, OWN), :] += jnp.dot(tile, rows, preferred_element_type=jnp.float32)

    def take(i, _):
        j = spread(i // SIDE) * SIDE + spread(lax.rem(i, SIDE))
        box_copy(j).wait_recv()
        acc[pl.ds(0, OWN), :] += inbox[j].astype(jnp.float32)
        return 0

    lax.fori_loop(0, 15, take, 0)
    out[...] = acc[pl.ds(0, OWN), :]

    def drain(j, _):
        row_copy(j).wait_send()
        box_copy(j).wait_send()
        return 0

    lax.fori_loop(1, 16, drain, 0)
    for q in range(5):
        for dy in range(4):
            on_chip(dy, q).wait_send()
        upward(0, q).wait_send()
        downward(0, q).wait_send()
    for q in (4, 0, 1):
        upward(1, q).wait_send()
    for q in (2, 3):
        downward(3, q).wait_send()


def sample_rows(probes, points, gain):
    bf16, f32, dma = jnp.bfloat16, jnp.float32, pltpu.SemaphoreType.DMA
    rows = 16 * OWN
    return pl.pallas_call(
        partial(sample_kernel, gain),
        out_shape=jax.ShapeDtypeStruct((OWN, 256), f32),
        in_specs=[pl.BlockSpec(memory_space=pl.ANY), pl.BlockSpec(memory_space=pl.ANY)],
        out_specs=pl.BlockSpec(memory_space=pltpu.VMEM),
        scratch_shapes=[
            pltpu.VMEM((8 * CHUNK, 256), bf16),
            pltpu.VMEM((8, 4, 16, OWN), bf16),
            pltpu.VMEM((16, 16, OWN), bf16),
            pltpu.VMEM((FEATS, 8 * CHUNK), bf16),
            pltpu.VMEM((rows, FEATS), bf16),
            pltpu.VMEM((rows, 256), f32),
            pltpu.VMEM((16, OWN, 256), bf16),
            pltpu.VMEM((16, OWN, 256), bf16),
            dma((6,)), dma((16,)), dma((16,)), dma((4, 5)), dma((2, 5)), dma((2, 5)), dma((8, 5)), dma((16,)), dma((16,)),
        ],
        compiler_params=pltpu.CompilerParams(collective_id=0, has_side_effects=True, vmem_limit_bytes=60 << 20),
    )(probes, points)


def swapped(value, axis, bit):
    return lax.ppermute(value, axis, [(i, i ^ 1 << bit) for i in range(lax.axis_size(axis))])


def couple(row_feats, col_feats, kernel_gain):
    cross = jnp.dot(row_feats.T, col_feats, precision=exact_mode)
    row_sq = jnp.sum(row_feats * row_feats, axis=0)
    col_sq = jnp.sum(col_feats * col_feats, axis=0)
    feat_count = row_feats.shape[0]
    return kernel_gain * jnp.exp(
        (2.0 * cross - row_sq[:, None] - col_sq[None, :]) / (2.0 * feat_count)
    )


def interpolate(stacked, chosen):
    skeleton = jnp.take(stacked, chosen, axis=0)
    gram_mat = jnp.dot(skeleton, skeleton.T, precision=exact_mode)
    damping = 0.05 * jnp.sum(skeleton * skeleton) / chosen.shape[0] + 1e-05
    factor = jnp.linalg.cholesky(gram_mat + damping * jnp.eye(chosen.shape[0], dtype=stacked.dtype))
    cross_mat = jnp.dot(stacked, skeleton.T, precision=exact_mode)
    solved = jax.scipy.linalg.cho_solve((factor, True), cross_mat.T)
    return (solved.T, skeleton)


def leaf_level(leaf_rows, leaf_probes, coords, chosen):
    interp, skeleton = interpolate(leaf_rows, chosen)
    reduced = jnp.dot(interp.T, leaf_probes.astype(interp.dtype), precision=exact_mode)
    picked = jnp.take(coords, chosen, axis=1).astype(jnp.float32)
    return (interp, (skeleton, reduced, picked))


def merge_pair(first_child, second_child, chosen, kernel_gain):
    first_samples, first_reduced, first_points = first_child
    second_samples, second_reduced, second_points = second_child
    upper_rows = first_samples - jnp.dot(
        couple(first_points, second_points, kernel_gain), second_reduced, precision=exact_mode
    )
    lower_rows = second_samples - jnp.dot(
        couple(second_points, first_points, kernel_gain), first_reduced, precision=exact_mode
    )
    stacked = jnp.concatenate([upper_rows, lower_rows], axis=0)
    interp, skeleton = interpolate(stacked, chosen)
    reduced = jnp.dot(
        interp.T, jnp.concatenate([first_reduced, second_reduced], axis=0), precision=exact_mode
    )
    joined = jnp.take(jnp.concatenate([first_points, second_points], axis=1), chosen, axis=1)
    return (interp, (skeleton, reduced, joined))


def take_first(values):
    return values[0]


def take_second(values):
    return values[1]


def local(probes, points, leaf_skeleton, skeleton_one, skeleton_two, skeleton_three):
    feat_count = points.shape[0]
    own_rows = probes.shape[1]
    col_pos = lax.axis_index("col")
    extent = own_rows * lax.axis_size("row") * lax.axis_size("col")
    kernel_gain = 16.0 / math.sqrt(4 * extent)
    owned = sample_rows(probes, points.transpose(1, 0, 2), kernel_gain)
    leaf_count = own_rows // LEAF
    leaf_rows = owned.reshape(leaf_count, LEAF, -1)
    leaf_probes = probes[0].reshape(leaf_count, LEAF, -1)
    leaf_coords = points[:, 0].reshape(feat_count, leaf_count, LEAF).transpose(1, 0, 2)
    leaf_interp, carried = jax.vmap(leaf_level)(leaf_rows, leaf_probes, leaf_coords, leaf_skeleton)
    first_child = jax.tree.map(take_first, carried)
    second_child = jax.tree.map(take_second, carried)
    interp_one, carried = merge_pair(first_child, second_child, skeleton_one[0], kernel_gain)
    upper_list = [interp_one]
    for bit_num in range(2):
        partner = swapped((carried[0], carried[1], carried[2]), "col", bit_num)
        mine_first = col_pos >> bit_num & 1 == 0
        first_child = jax.tree.map(partial(jnp.where, mine_first), carried, partner)
        second_child = jax.tree.map(partial(jnp.where, mine_first), partner, carried)
        table_rows = skeleton_two if bit_num == 0 else skeleton_three
        chosen = lax.dynamic_index_in_dim(table_rows, col_pos // (2 << bit_num), 0, keepdims=False)
        interp_up, carried = merge_pair(first_child, second_child, chosen, kernel_gain)
        upper_list.append(interp_up)
    upper_interp = jnp.stack(upper_list)[:, None]
    top_state = jnp.stack([carried[0], carried[1]])[:, None]
    return (leaf_interp, upper_interp, top_state)


def solution(mesh):
    placed = (
        P(None, ("row", "col"), None),
        P(None, None, ("row", "col")),
        P(("row", "col"), None),
        P(("row", "col"), None),
        P("row", None),
        P("row", None),
    )
    return jax.shard_map(
        local,
        mesh=mesh,
        in_specs=placed,
        out_specs=(
            P(("row", "col"), None, None),
            P(None, ("row", "col"), None, None),
            P(None, ("row", "col"), None, None),
        ),
        check_vma=False,
    )
```

```python
from functools import partial
import math

import jax
import jax.numpy as jnp
from jax import lax
from jax.experimental import pallas as pl
from jax.experimental.pallas import tpu as pltpu
from jax.sharding import PartitionSpec as P

LEAF = 128
MESH = pl.DeviceIdType.MESH
exact_mode = lax.Precision.HIGHEST
LOG2E = math.log2(math.e)
SIDE = 4
OWN = 256
CHUNK = 4 * OWN
FEATS = 64
PLACE = {(0, 0): 0, (0, 1): 1, (1, 0): 2, (3, 0): 3, (1, 1): 4, (3, 1): 5, (2, 0): 6, (2, 1): 7}
EARLY = 3


def pieces(value):
    high = value.astype(jnp.bfloat16).astype(jnp.float32)
    rest = value - high
    mid = rest.astype(jnp.bfloat16).astype(jnp.float32)
    return high, mid, rest - mid


def extra_rows(first, second, width=OWN):
    row = lax.broadcasted_iota(jnp.int32, (16, width), 0)
    out = jnp.zeros((16, width), jnp.float32)
    for i, value in enumerate((*first, *second)):
        out = jnp.where(row == i, value, out)
    return out


def exact(a, b, dims=((1,), (0,))):
    return lax.dot_general(a, b, (dims, ((), ())), precision=exact_mode, preferred_element_type=jnp.float32)

def split(v):
    h = v.astype(jnp.bfloat16)
    r = v - h.astype(jnp.float32)
    m = r.astype(jnp.bfloat16)
    return h, m, (r - m.astype(jnp.float32)).astype(jnp.bfloat16)

def select_rows(pick, values):
    return jnp.dot(jnp.concatenate([pick] * 3, axis=1), jnp.concatenate(split(values), axis=0), preferred_element_type=jnp.float32)

def pick_of(chosen):
    hits = lax.broadcasted_iota(jnp.int32, (128, 64), 0) == chosen
    return hits.astype(jnp.float32).T.astype(jnp.bfloat16)

def wide(col, width):
    return jnp.concatenate([col, col[:, :width - 128]], axis=1) if width > 128 else col[:, :width]

def eliminate(systems):
    width = systems[0].shape[1]
    sub = lax.broadcasted_iota(jnp.int32, (8, 1), 0)
    systems = [[m[8 * i:8 * i + 8, :] for i in range(8)] for m in systems]
    for b in range(8):
        for m in systems:
            cols = [[jnp.broadcast_to(m[i][:, 8 * b + j:8 * b + j + 1], (8, 128)) for j in range(8)] for i in range(8)]
            p, lead = m[b], list(cols[b])
            for k in range(8):
                inv = 1.0 / lead[k][k:k + 1, :]
                f = lead[k] * inv
                q = p[k:k + 1, :]
                p = jnp.where(sub == k, q * wide(inv, width), p - wide(f, width) * q)
                for j in range(k + 1, 8):
                    q = lead[j][k:k + 1, :]
                    lead[j] = jnp.where(sub == k, q * inv, lead[j] - f * q)
            m[b] = p
            for i in range(8):
                if i != b:
                    total = m[i]
                    for k in range(8):
                        total = total - wide(cols[i][k], width) * p[k:k + 1, :]
                    m[i] = total
    return [jnp.concatenate(m, axis=0)[:, 64:] for m in systems]

def interpolate(stacked, picks, keep=None):
    systems, kept = [], []
    eye = lax.broadcasted_iota(jnp.int32, (64, 64), 0) == lax.broadcasted_iota(jnp.int32, (64, 64), 1)
    for y, pick in zip(stacked, picks):
        z = select_rows(pick, y)
        kept.append(z)
        if keep is not None:
            keep(z)
        cross = exact(z, y, ((1,), (1,)))
        gram = lax.dot_general(jnp.concatenate(split(cross), axis=1), jnp.concatenate([pick] * 3, axis=1), (((1,), (1,)), ((), ())), preferred_element_type=jnp.float32)
        diag = jnp.where(eye, gram, 0.0)
        ridge = jnp.sum(diag, keepdims=True) * (0.05 / 64) + 1e-5
        gram = gram + jnp.where(eye, ridge, 0.0)
        systems.append(jnp.concatenate([gram, cross], axis=1))
    return eliminate(systems), kept


def kernel_square(gain, feats):
    sq = jnp.sum(feats * feats, axis=0, keepdims=True)
    ones = (jnp.ones((1, 128), jnp.float32),) * 3
    left = jnp.concatenate([*pieces(feats * (LOG2E / 16)), extra_rows(pieces(math.log2(gain) - sq * (LOG2E / 32)), ones, 128)], axis=0)
    right = jnp.concatenate([feats, feats, feats, extra_rows(ones, pieces(sq * (-LOG2E / 32)), 128)], axis=0)
    power = jnp.dot(left.T.astype(jnp.bfloat16), right.astype(jnp.bfloat16), preferred_element_type=jnp.float32)
    child = lax.broadcasted_iota(jnp.int32, (128, 128), 0) // 64
    other = lax.broadcasted_iota(jnp.int32, (128, 128), 1) // 64
    return jnp.where(child == other, 0.0, jnp.exp2(power))


def spread(i):
    return lax.rem(2 + i + lax.div(i * (i - 1), 2), SIDE)


def hss_kernel(gain, probes, points, chosen_leaf, chosen_one, chosen_two, chosen_three, leaf_out, upper_out, top_out,
               prb, pts, rpts, colf, rowf, acc, outbox, inbox, picks, square, pair_p, pair_z, pair_r, leaf_x, upper_x, top_x,
               loc_sem, rp_send, rp_recv, chip_send, up_send, down_send, got, box_send, box_recv, pair_send, pair_recv, out_sem):
    row, col = lax.axis_index("row"), lax.axis_index("col")
    y, core = row // 2, lax.rem(row, 2)
    x, z = col // SIDE, lax.rem(col, SIDE)
    up = lax.rem(y + 1, SIDE) * 2 + core
    down = lax.rem(y + 3, SIDE) * 2 + core
    partner = y * 2 + 1 - core

    local = [pltpu.make_async_copy(probes.at[q], prb.at[pl.ds(q * OWN, OWN)], loc_sem.at[q]) for q in range(4)]
    local.append(pltpu.make_async_copy(points, pts.at[0], loc_sem.at[4]))
    local.append(pltpu.make_async_copy(points.at[0], rpts.at[0], loc_sem.at[5]))
    for copy in local:
        copy.start()

    def peer_col(j, sign):
        dx, dz = j // SIDE, lax.rem(j, SIDE)
        return lax.rem(x + sign * dx + SIDE, SIDE) * SIDE + lax.rem(z + sign * dz + SIDE, SIDE)

    barrier = pltpu.get_barrier_semaphore()
    for other in (up, down, partner):
        pl.semaphore_signal(barrier, inc=1, device_id=(other, col), device_id_type=MESH)

    def greet(j, _):
        pl.semaphore_signal(barrier, inc=1, device_id=(row, peer_col(j, 1)), device_id_type=MESH)
        return 0

    lax.fori_loop(1, 16, greet, 0)
    for copy in local:
        copy.wait()

    bits = (lax.rem(col, 2), lax.rem(col // 2, 2))

    def pair_copy(level, kind):
        bit = bits[level]
        ref = pair_p.at[level, bit] if kind == 0 else (pair_z, pair_r)[kind - 1].at[level, pl.ds(pl.multiple_of(bit * 64, 64), 64)]
        return pltpu.make_async_remote_copy(
            src_ref=ref, dst_ref=ref, send_sem=pair_send.at[level, kind], recv_sem=pair_recv.at[level, kind],
            device_id=(row, col + (1 - 2 * bit) * (level + 1)), device_id_type=MESH)

    for leaf in range(2):
        picks[leaf] = pick_of(chosen_leaf[leaf:leaf + 1, :])
    picks[2] = pick_of(chosen_one[...])
    picks[3] = pick_of(chosen_two[pl.ds(col // 2, 1), :])
    picks[4] = pick_of(chosen_three[pl.ds(col // 4, 1), :])

    def picked(feats, pick):
        return lax.dot_general(feats, pick, (((1,), (1,)), ((), ())), preferred_element_type=jnp.float32)

    def child_points(level, feats):
        square[level] = kernel_square(gain, feats)
        if level < 2:
            pair_p[level, bits[level]] = picked(feats.astype(jnp.bfloat16), picks[2 + level]).astype(jnp.bfloat16)

    def pair_points(level):
        pair_copy(level, 0).wait_recv()
        return jnp.concatenate([pair_p[level, 0], pair_p[level, 1]], axis=1).astype(jnp.float32)

    child_points(0, jnp.concatenate([picked(pts[0, 0, :, leaf * LEAF:(leaf + 1) * LEAF], picks[leaf]) for leaf in range(2)], axis=1))
    pl.semaphore_wait(barrier, 18)

    def row_copy(j):
        return pltpu.make_async_remote_copy(
            src_ref=rpts.at[0], dst_ref=rpts.at[j], send_sem=rp_send.at[j], recv_sem=rp_recv.at[j],
            device_id=(row, peer_col(j, 1)), device_id_type=MESH)

    def send_row(j, _):
        row_copy(j).start()
        return 0

    def piece_copy(src, dst, q, sem, target):
        src_ref = pts.at[src] if q == 4 else prb.at[pl.ds(src * CHUNK + q * OWN, OWN)]
        dst_ref = pts.at[dst] if q == 4 else prb.at[pl.ds(dst * CHUNK + q * OWN, OWN)]
        return pltpu.make_async_remote_copy(
            src_ref=src_ref, dst_ref=dst_ref, send_sem=sem, recv_sem=got.at[dst, q],
            device_id=(target, col), device_id_type=MESH)

    def on_chip(dy, q):
        return piece_copy(PLACE[dy, 0], PLACE[dy, 1], q, chip_send.at[dy, q], partner)

    def upward(src_dy, q):
        return piece_copy(PLACE[src_dy, 0], PLACE[src_dy + 1, 0], q, up_send.at[src_dy, q], up)

    def downward(src_dy, q):
        return piece_copy(PLACE[src_dy, 0], PLACE[3 if src_dy == 0 else 2, 0], q, down_send.at[src_dy // 3, q], down)

    def arrived(dy, dc, q):
        place = PLACE[dy, dc]
        piece_copy(place, place, q, chip_send.at[0, 0], partner).wait_recv()

    on_chip(0, 4).start()
    upward(0, 4).start()
    downward(0, 4).start()
    lax.fori_loop(1, 16, send_row, 0)
    pair_copy(0, 0).start()
    for q in range(4):
        on_chip(0, q).start()
    for q, r in zip((0, 1, 2, 3), (2, 3, 0, 1)):
        upward(0, q).start()
        downward(0, r).start()

    def col_features(place):
        for q in range(4):
            feats = pts[place, q].astype(jnp.float32)
            bias = jnp.sum(feats * feats, axis=0, keepdims=True) * (-LOG2E / 32)
            ones = (jnp.float32(1),) * 3
            stacked = jnp.concatenate([feats, feats, feats, extra_rows(ones, pieces(bias))], axis=0)
            colf[:, pl.ds(place * CHUNK + q * OWN, OWN)] = stacked.astype(jnp.bfloat16)

    def row_features(j):
        feats = rpts[j].astype(jnp.float32)
        bias = math.log2(gain) - jnp.sum(feats * feats, axis=0, keepdims=True) * (LOG2E / 32)
        ones = (jnp.float32(1),) * 3
        stacked = jnp.concatenate([*pieces(feats * (LOG2E / 16)), extra_rows(pieces(bias), ones)], axis=0)
        rowf[pl.ds(pl.multiple_of(j * OWN, OWN), OWN), :] = stacked.T.astype(jnp.bfloat16)

    def block(j, first, last):
        rows = rowf[pl.ds(pl.multiple_of(j * OWN, OWN), OWN), :]
        cols = pl.ds(first * CHUNK, (last - first) * CHUNK)
        power = jnp.dot(rows, colf[:, cols], preferred_element_type=jnp.float32)
        return jnp.exp2(power).astype(jnp.bfloat16), prb[cols, :]

    def at(j):
        return pl.ds(pl.multiple_of(j * OWN, OWN), OWN)

    col_features(0)
    row_features(0)
    power = jnp.dot(rowf[pl.ds(0, OWN), :], colf[:, pl.ds(0, CHUNK)], preferred_element_type=jnp.float32)
    leaf_of = lax.broadcasted_iota(jnp.int32, (OWN, CHUNK), 0) // LEAF
    other_leaf = lax.broadcasted_iota(jnp.int32, (OWN, CHUNK), 1) // LEAF
    tile = jnp.where(leaf_of == other_leaf, 0.0, jnp.exp2(power)).astype(jnp.bfloat16)
    own_sum = jnp.dot(tile, prb[pl.ds(0, CHUNK), :], preferred_element_type=jnp.float32)
    for q in (4, 0, 1, 2, 3):
        arrived(0, 1, q)
    col_features(1)
    tile, rows = block(0, 1, 2)
    acc[pl.ds(0, OWN), :] = own_sum + jnp.dot(tile, rows, preferred_element_type=jnp.float32)

    def near_block(j, _):
        row_copy(j).wait_recv()
        row_features(j)
        tile, rows = block(j, 0, 2)
        acc[at(j), :] = jnp.dot(tile, rows, preferred_element_type=jnp.float32)

        @pl.when(j == 10)
        def _():
            for q in (4, 0, 1):
                arrived(1, 0, q)
                upward(1, q).start()
                on_chip(1, q).start()
            for q in (4, 2, 3):
                arrived(3, 0, q)
                if q != 4:
                    downward(3, q).start()
                on_chip(3, q).start()
        return 0

    lax.fori_loop(1, 16, near_block, 0)
    for q, r in ((2, 0), (3, 1)):
        arrived(1, 0, q)
        on_chip(1, q).start()
        arrived(3, 0, r)
        on_chip(3, r).start()
    for place in range(2, EARLY):
        col_features(place)
    child_points(1, pair_points(0))
    pair_copy(1, 0).start()

    def mid_block(j, _):
        tile, rows = block(j, 2, EARLY)
        acc[at(j), :] += jnp.dot(tile, rows, preferred_element_type=jnp.float32)

        @pl.when(j == 12)
        def _():
            for q in (4, 0, 2, 1, 3):
                arrived(2, 0, q)
                on_chip(2, q).start()
        return 0

    lax.fori_loop(0, 16, mid_block, 0)
    child_points(2, pair_points(1))
    for dy in (1, 3, 2):
        for q in (4, 0, 1, 2, 3):
            arrived(dy, 1, q)
    for place in range(EARLY, 8):
        col_features(place)

    def box_copy(j):
        return pltpu.make_async_remote_copy(
            src_ref=outbox.at[j], dst_ref=inbox.at[j], send_sem=box_send.at[j], recv_sem=box_recv.at[j],
            device_id=(row, peer_col(j, -1)), device_id_type=MESH)

    def last_block(i, _):
        j = spread(i // SIDE) * SIDE + spread(lax.rem(i, SIDE))
        tile, rows = block(j, EARLY, 8)
        total = acc[at(j), :] + jnp.dot(tile, rows, preferred_element_type=jnp.float32)
        outbox[j] = total.astype(jnp.bfloat16)
        box_copy(j).start()
        return 0

    lax.fori_loop(0, 15, last_block, 0)
    tile, rows = block(0, EARLY, 8)
    acc[pl.ds(0, OWN), :] += jnp.dot(tile, rows, preferred_element_type=jnp.float32)

    def take(i, _):
        j = spread(i // SIDE) * SIDE + spread(lax.rem(i, SIDE))
        box_copy(j).wait_recv()
        acc[pl.ds(0, OWN), :] += inbox[j].astype(jnp.float32)
        return 0

    lax.fori_loop(0, 15, take, 0)

    def leave(src, dst, sem):
        pltpu.make_async_copy(src, dst, sem).start()

    solved, kept = interpolate([acc[pl.ds(leaf * LEAF, LEAF), :] for leaf in range(2)], [picks[0], picks[1]])
    reduced = []
    for leaf, value in enumerate(solved):
        rows = prb[pl.ds(leaf * LEAF, LEAF), :]
        reduced.append(jnp.dot(jnp.concatenate(split(value), axis=1), jnp.concatenate([rows] * 3, axis=0), preferred_element_type=jnp.float32))
        leaf_x[leaf] = value.T
    leave(leaf_x, leaf_out, out_sem.at[0])
    below, weights = jnp.concatenate(kept, axis=0), jnp.concatenate(reduced, axis=0)
    for level in range(3):
        if level > 0:
            pair_copy(level - 1, 1).wait_recv()
            pair_copy(level - 1, 2).wait_recv()
            below, weights = pair_z[level - 1], pair_r[level - 1]

        def keep(value):
            if level == 2:
                top_x[0] = value
            else:
                pair_z[level, pl.ds(pl.multiple_of(bits[level] * 64, 64), 64), :] = value
                pair_copy(level, 1).start()

        solved, _ = interpolate([below - exact(square[level], weights)], [picks[2 + level]], keep)
        value = exact(solved[0], weights)
        if level == 2:
            top_x[1] = value
            leave(top_x, top_out, out_sem.at[4])
        else:
            pair_r[level, pl.ds(pl.multiple_of(bits[level] * 64, 64), 64), :] = value
            pair_copy(level, 2).start()
        upper_x[level] = solved[0].T
        leave(upper_x.at[level], upper_out.at[level], out_sem.at[1 + level])

    def drain(j, _):
        row_copy(j).wait_send()
        box_copy(j).wait_send()
        return 0

    lax.fori_loop(1, 16, drain, 0)
    for q in range(5):
        for dy in range(4):
            on_chip(dy, q).wait_send()
        upward(0, q).wait_send()
        downward(0, q).wait_send()
    for q in (4, 0, 1):
        upward(1, q).wait_send()
    for q in (2, 3):
        downward(3, q).wait_send()
    for level in range(2):
        for kind in range(3):
            pair_copy(level, kind).wait_send()
    pltpu.make_async_copy(leaf_x, leaf_out, out_sem.at[0]).wait()
    for level in range(3):
        pltpu.make_async_copy(upper_x.at[level], upper_out.at[level], out_sem.at[1 + level]).wait()
    pltpu.make_async_copy(top_x, top_out, out_sem.at[4]).wait()


def local(probes, points, leaf_skeleton, skeleton_one, skeleton_two, skeleton_three):
    bf16, f32, dma, vmem = jnp.bfloat16, jnp.float32, pltpu.SemaphoreType.DMA, pltpu.VMEM
    extent = OWN * lax.axis_size("row") * lax.axis_size("col")
    kernel_gain = 16.0 / math.sqrt(4 * extent)
    rows = 16 * OWN
    outside, inside = pl.BlockSpec(memory_space=pl.ANY), pl.BlockSpec(memory_space=vmem)
    leaf_interp, upper_interp, top_state = pl.pallas_call(
        partial(hss_kernel, kernel_gain),
        out_shape=(
            jax.ShapeDtypeStruct((2, LEAF, 64), f32),
            jax.ShapeDtypeStruct((3, LEAF, 64), f32),
            jax.ShapeDtypeStruct((2, 64, 256), f32),
        ),
        in_specs=[outside, outside, inside, inside, inside, inside],
        out_specs=(outside, outside, outside),
        scratch_shapes=[
            vmem((8 * CHUNK, 256), bf16),
            vmem((8, 4, 16, OWN), bf16),
            vmem((16, 16, OWN), bf16),
            vmem((FEATS, 8 * CHUNK), bf16),
            vmem((rows, FEATS), bf16),
            vmem((rows, 256), f32),
            vmem((16, OWN, 256), bf16),
            vmem((16, OWN, 256), bf16),
            vmem((5, 64, LEAF), bf16),
            vmem((3, LEAF, LEAF), f32),
            vmem((2, 2, 16, 64), bf16),
            vmem((2, LEAF, 256), f32),
            vmem((2, LEAF, 256), f32),
            vmem((2, LEAF, 64), f32),
            vmem((3, LEAF, 64), f32),
            vmem((2, 64, 256), f32),
            dma((6,)), dma((16,)), dma((16,)), dma((4, 5)), dma((2, 5)), dma((2, 5)), dma((8, 5)), dma((16,)), dma((16,)),
            dma((2, 3)), dma((2, 3)), dma((5,)),
        ],
        compiler_params=pltpu.CompilerParams(collective_id=0, has_side_effects=True, vmem_limit_bytes=60 << 20),
    )(probes, points.transpose(1, 0, 2), leaf_skeleton, skeleton_one, skeleton_two, skeleton_three)
    return leaf_interp, upper_interp[:, None], top_state[:, None]


def solution(mesh):
    placed = (
        P(None, ("row", "col"), None),
        P(None, None, ("row", "col")),
        P(("row", "col"), None),
        P(("row", "col"), None),
        P("row", None),
        P("row", None),
    )
    return jax.shard_map(
        local,
        mesh=mesh,
        in_specs=placed,
        out_specs=(
            P(("row", "col"), None, None),
            P(None, ("row", "col"), None, None),
            P(None, ("row", "col"), None, None),
        ),
        check_vma=False,
    )
```

```python
from functools import partial
import math

import jax
import jax.numpy as jnp
from jax import lax
from jax.experimental import pallas as pl
from jax.experimental.pallas import tpu as pltpu
from jax.sharding import PartitionSpec as P

LEAF = 128
MESH = pl.DeviceIdType.MESH
exact_mode = lax.Precision.HIGHEST
LOG2E = math.log2(math.e)
SIDE = 4
OWN = 256
CHUNK = 4 * OWN
FEATS = 64
PLACE = {(0, 0): 0, (0, 1): 1, (1, 0): 2, (3, 0): 3, (1, 1): 4, (3, 1): 5, (2, 0): 6, (2, 1): 7}
EARLY = 3


def pieces(value):
    high = value.astype(jnp.bfloat16).astype(jnp.float32)
    rest = value - high
    mid = rest.astype(jnp.bfloat16).astype(jnp.float32)
    return high, mid, rest - mid


def extra_rows(first, second, width=OWN):
    row = lax.broadcasted_iota(jnp.int32, (16, width), 0)
    out = jnp.zeros((16, width), jnp.float32)
    for i, value in enumerate((*first, *second)):
        out = jnp.where(row == i, value, out)
    return out


def exact(a, b, dims=((1,), (0,))):
    return lax.dot_general(a, b, (dims, ((), ())), precision=exact_mode, preferred_element_type=jnp.float32)

def split(v):
    h = v.astype(jnp.bfloat16)
    r = v - h.astype(jnp.float32)
    m = r.astype(jnp.bfloat16)
    return h, m, (r - m.astype(jnp.float32)).astype(jnp.bfloat16)

def select_rows(pick, values):
    return jnp.dot(jnp.concatenate([pick] * 3, axis=1), jnp.concatenate(split(values), axis=0), preferred_element_type=jnp.float32)

def pick_of(chosen):
    hits = lax.broadcasted_iota(jnp.int32, (128, 64), 0) == chosen
    return hits.astype(jnp.float32).T.astype(jnp.bfloat16)

def wide(col, width):
    return jnp.concatenate([col, col[:, :width - 128]], axis=1) if width > 128 else col[:, :width]

def eliminate(systems):
    width = systems[0].shape[1]
    sub = lax.broadcasted_iota(jnp.int32, (8, 1), 0)
    systems = [[m[8 * i:8 * i + 8, :] for i in range(8)] for m in systems]
    for b in range(8):
        for m in systems:
            cols = [[jnp.broadcast_to(m[i][:, 8 * b + j:8 * b + j + 1], (8, 128)) for j in range(8)] for i in range(8)]
            p, lead = m[b], list(cols[b])
            for k in range(8):
                inv = 1.0 / lead[k][k:k + 1, :]
                f = lead[k] * inv
                q = p[k:k + 1, :]
                p = jnp.where(sub == k, q * wide(inv, width), p - wide(f, width) * q)
                for j in range(k + 1, 8):
                    q = lead[j][k:k + 1, :]
                    lead[j] = jnp.where(sub == k, q * inv, lead[j] - f * q)
            m[b] = p
            for i in range(8):
                if i != b:
                    total = m[i]
                    for k in range(8):
                        total = total - wide(cols[i][k], width) * p[k:k + 1, :]
                    m[i] = total
    return [jnp.concatenate(m, axis=0)[:, 64:] for m in systems]

def interpolate(stacked, picks, keep=None):
    systems, kept = [], []
    eye = lax.broadcasted_iota(jnp.int32, (64, 64), 0) == lax.broadcasted_iota(jnp.int32, (64, 64), 1)
    for y, pick in zip(stacked, picks):
        z = select_rows(pick, y)
        kept.append(z)
        if keep is not None:
            keep(z)
        cross = exact(z, y, ((1,), (1,)))
        gram = lax.dot_general(jnp.concatenate(split(cross), axis=1), jnp.concatenate([pick] * 3, axis=1), (((1,), (1,)), ((), ())), preferred_element_type=jnp.float32)
        diag = jnp.where(eye, gram, 0.0)
        ridge = jnp.sum(diag, keepdims=True) * (0.05 / 64) + 1e-5
        gram = gram + jnp.where(eye, ridge, 0.0)
        systems.append(jnp.concatenate([gram, cross], axis=1))
    return eliminate(systems), kept


def kernel_square(gain, feats):
    sq = jnp.sum(feats * feats, axis=0, keepdims=True)
    ones = (jnp.ones((1, 128), jnp.float32),) * 3
    left = jnp.concatenate([*pieces(feats * (LOG2E / 16)), extra_rows(pieces(math.log2(gain) - sq * (LOG2E / 32)), ones, 128)], axis=0)
    right = jnp.concatenate([feats, feats, feats, extra_rows(ones, pieces(sq * (-LOG2E / 32)), 128)], axis=0)
    power = jnp.dot(left.T.astype(jnp.bfloat16), right.astype(jnp.bfloat16), preferred_element_type=jnp.float32)
    child = lax.broadcasted_iota(jnp.int32, (128, 128), 0) // 64
    other = lax.broadcasted_iota(jnp.int32, (128, 128), 1) // 64
    return jnp.where(child == other, 0.0, jnp.exp2(power))


def hss_kernel(gain, probes, points, chosen_leaf, chosen_one, chosen_two, chosen_three, leaf_out, upper_out, top_out,
               prb, pts, rpts, colf, rowf, acc, outbox, inbox, picks, square, pair_p, pair_z, pair_r, leaf_x, upper_x, top_x,
               loc_sem, rp_send, rp_recv, chip_send, up_send, down_send, got, box_send, box_recv, pair_send, pair_recv, out_sem):
    row, col = lax.axis_index("row"), lax.axis_index("col")
    y, core = row // 2, lax.rem(row, 2)
    x, z = col // SIDE, lax.rem(col, SIDE)
    up = lax.rem(y + 1, SIDE) * 2 + core
    down = lax.rem(y + 3, SIDE) * 2 + core
    partner = y * 2 + 1 - core

    local = [pltpu.make_async_copy(probes.at[q], prb.at[pl.ds(q * OWN, OWN)], loc_sem.at[q]) for q in range(4)]
    for copy in local:
        copy.start()
    feats = points[...].astype(jnp.float32)
    for q in range(4):
        pts[0, q] = feats[:, q, :].astype(jnp.bfloat16)
    rpts[0] = pts[0, 0]

    def peer_col(j, sign):
        dx, dz = j // SIDE, lax.rem(j, SIDE)
        return lax.rem(x + sign * dx + SIDE, SIDE) * SIDE + lax.rem(z + sign * dz + SIDE, SIDE)

    barrier = pltpu.get_barrier_semaphore()
    for other in (up, down, partner):
        pl.semaphore_signal(barrier, inc=1, device_id=(other, col), device_id_type=MESH)

    def greet(j, _):
        pl.semaphore_signal(barrier, inc=1, device_id=(row, peer_col(j, 1)), device_id_type=MESH)
        return 0

    lax.fori_loop(1, 16, greet, 0)
    for copy in local:
        copy.wait()

    bits = (lax.rem(col, 2), lax.rem(col // 2, 2))

    def pair_copy(level, kind):
        bit = bits[level]
        ref = pair_p.at[level, bit] if kind == 0 else (pair_z, pair_r)[kind - 1].at[level, pl.ds(pl.multiple_of(bit * 64, 64), 64)]
        return pltpu.make_async_remote_copy(
            src_ref=ref, dst_ref=ref, send_sem=pair_send.at[level, kind], recv_sem=pair_recv.at[level, kind],
            device_id=(row, col + (1 - 2 * bit) * (level + 1)), device_id_type=MESH)

    for leaf in range(2):
        picks[leaf] = pick_of(chosen_leaf[leaf:leaf + 1, :])
    picks[2] = pick_of(chosen_one[...])
    picks[3] = pick_of(chosen_two[pl.ds(col // 2, 1), :])
    picks[4] = pick_of(chosen_three[pl.ds(col // 4, 1), :])

    def picked(feats, pick):
        return lax.dot_general(feats, pick, (((1,), (1,)), ((), ())), preferred_element_type=jnp.float32)

    def child_points(level, feats):
        square[level] = kernel_square(gain, feats)
        if level < 2:
            pair_p[level, bits[level]] = picked(feats.astype(jnp.bfloat16), picks[2 + level]).astype(jnp.bfloat16)

    def pair_points(level):
        pair_copy(level, 0).wait_recv()
        return jnp.concatenate([pair_p[level, 0], pair_p[level, 1]], axis=1).astype(jnp.float32)

    child_points(0, jnp.concatenate([picked(pts[0, 0, :, leaf * LEAF:(leaf + 1) * LEAF], picks[leaf]) for leaf in range(2)], axis=1))
    pl.semaphore_wait(barrier, 18)

    def row_copy(j):
        return pltpu.make_async_remote_copy(
            src_ref=rpts.at[0], dst_ref=rpts.at[j], send_sem=rp_send.at[j], recv_sem=rp_recv.at[j],
            device_id=(row, peer_col(j, 1)), device_id_type=MESH)

    def send_row(j, _):
        row_copy(j).start()
        return 0

    def piece_copy(src, dst, q, sem, target):
        src_ref = pts.at[src] if q == 4 else prb.at[pl.ds(src * CHUNK + q * OWN, OWN)]
        dst_ref = pts.at[dst] if q == 4 else prb.at[pl.ds(dst * CHUNK + q * OWN, OWN)]
        return pltpu.make_async_remote_copy(
            src_ref=src_ref, dst_ref=dst_ref, send_sem=sem, recv_sem=got.at[dst, q],
            device_id=(target, col), device_id_type=MESH)

    def on_chip(dy, q):
        return piece_copy(PLACE[dy, 0], PLACE[dy, 1], q, chip_send.at[dy, q], partner)

    def upward(src_dy, q):
        return piece_copy(PLACE[src_dy, 0], PLACE[src_dy + 1, 0], q, up_send.at[src_dy, q], up)

    def downward(src_dy, q):
        return piece_copy(PLACE[src_dy, 0], PLACE[3 if src_dy == 0 else 2, 0], q, down_send.at[src_dy // 3, q], down)

    def arrived(dy, dc, q):
        place = PLACE[dy, dc]
        piece_copy(place, place, q, chip_send.at[0, 0], partner).wait_recv()

    on_chip(0, 4).start()
    upward(0, 4).start()
    downward(0, 4).start()
    lax.fori_loop(1, 16, send_row, 0)
    pair_copy(0, 0).start()
    for q in range(4):
        on_chip(0, q).start()
    for q, r in zip((0, 1, 2, 3), (2, 3, 0, 1)):
        upward(0, q).start()
        downward(0, r).start()

    def col_features(place):
        for q in range(4):
            feats = pts[place, q].astype(jnp.float32)
            bias = jnp.sum(feats * feats, axis=0, keepdims=True) * (-LOG2E / 32)
            ones = (jnp.float32(1),) * 3
            stacked = jnp.concatenate([feats, feats, feats, extra_rows(ones, pieces(bias))], axis=0)
            colf[:, pl.ds(place * CHUNK + q * OWN, OWN)] = stacked.astype(jnp.bfloat16)

    def row_features(j):
        feats = rpts[j].astype(jnp.float32)
        bias = math.log2(gain) - jnp.sum(feats * feats, axis=0, keepdims=True) * (LOG2E / 32)
        ones = (jnp.float32(1),) * 3
        stacked = jnp.concatenate([*pieces(feats * (LOG2E / 16)), extra_rows(pieces(bias), ones)], axis=0)
        rowf[pl.ds(pl.multiple_of(j * OWN, OWN), OWN), :] = stacked.T.astype(jnp.bfloat16)

    def block(j, first, last):
        rows = rowf[pl.ds(pl.multiple_of(j * OWN, OWN), OWN), :]
        cols = pl.ds(first * CHUNK, (last - first) * CHUNK)
        power = jnp.dot(rows, colf[:, cols], preferred_element_type=jnp.float32)
        return jnp.exp2(power).astype(jnp.bfloat16), prb[cols, :]

    def at(j):
        return pl.ds(pl.multiple_of(j * OWN, OWN), OWN)

    col_features(0)
    row_features(0)
    power = jnp.dot(rowf[pl.ds(0, OWN), :], colf[:, pl.ds(0, CHUNK)], preferred_element_type=jnp.float32)
    leaf_of = lax.broadcasted_iota(jnp.int32, (OWN, CHUNK), 0) // LEAF
    other_leaf = lax.broadcasted_iota(jnp.int32, (OWN, CHUNK), 1) // LEAF
    tile = jnp.where(leaf_of == other_leaf, 0.0, jnp.exp2(power)).astype(jnp.bfloat16)
    own_sum = jnp.dot(tile, prb[pl.ds(0, CHUNK), :], preferred_element_type=jnp.float32)
    for q in (4, 0, 1, 2, 3):
        arrived(0, 1, q)
    col_features(1)
    tile, rows = block(0, 1, 2)
    acc[pl.ds(0, OWN), :] = own_sum + jnp.dot(tile, rows, preferred_element_type=jnp.float32)

    def near_block(j, _):
        row_copy(j).wait_recv()
        row_features(j)
        tile, rows = block(j, 0, 2)
        acc[at(j), :] = jnp.dot(tile, rows, preferred_element_type=jnp.float32)

        @pl.when(j == 10)
        def _():
            for q in (4, 0, 1):
                arrived(1, 0, q)
                upward(1, q).start()
                on_chip(1, q).start()
            for q in (4, 2, 3):
                arrived(3, 0, q)
                if q != 4:
                    downward(3, q).start()
                on_chip(3, q).start()
        return 0

    lax.fori_loop(1, 16, near_block, 0)
    for q, r in ((2, 0), (3, 1)):
        arrived(1, 0, q)
        on_chip(1, q).start()
        arrived(3, 0, r)
        on_chip(3, r).start()
    for place in range(2, EARLY):
        col_features(place)
    child_points(1, pair_points(0))
    pair_copy(1, 0).start()

    def mid_block(j, _):
        tile, rows = block(j, 2, EARLY)
        acc[at(j), :] += jnp.dot(tile, rows, preferred_element_type=jnp.float32)

        @pl.when(j == 12)
        def _():
            for q in (4, 0, 2, 1, 3):
                arrived(2, 0, q)
                on_chip(2, q).start()
        return 0

    lax.fori_loop(0, 16, mid_block, 0)
    child_points(2, pair_points(1))
    for dy in (1, 3, 2):
        for q in (4, 0, 1, 2, 3):
            arrived(dy, 1, q)
    for place in range(EARLY, 8):
        col_features(place)

    def box_copy(j):
        return pltpu.make_async_remote_copy(
            src_ref=outbox.at[j], dst_ref=inbox.at[j], send_sem=box_send.at[j], recv_sem=box_recv.at[j],
            device_id=(row, peer_col(j, -1)), device_id_type=MESH)

    def last_block(i, _):
        j = lax.rem(13 * i + 13, 16)
        tile, rows = block(j, EARLY, 8)
        total = acc[at(j), :] + jnp.dot(tile, rows, preferred_element_type=jnp.float32)
        outbox[j] = total.astype(jnp.bfloat16)
        box_copy(j).start()
        return 0

    lax.fori_loop(0, 15, last_block, 0)
    tile, rows = block(0, EARLY, 8)
    acc[pl.ds(0, OWN), :] += jnp.dot(tile, rows, preferred_element_type=jnp.float32)

    def take(i, _):
        j = lax.rem(13 * i + 13, 16)
        box_copy(j).wait_recv()
        acc[pl.ds(0, OWN), :] += inbox[j].astype(jnp.float32)
        return 0

    lax.fori_loop(0, 15, take, 0)

    def leave(src, dst, sem):
        pltpu.make_async_copy(src, dst, sem).start()

    solved, kept = interpolate([acc[pl.ds(leaf * LEAF, LEAF), :] for leaf in range(2)], [picks[0], picks[1]])
    reduced = []
    for leaf, value in enumerate(solved):
        rows = prb[pl.ds(leaf * LEAF, LEAF), :]
        reduced.append(jnp.dot(jnp.concatenate(split(value), axis=1), jnp.concatenate([rows] * 3, axis=0), preferred_element_type=jnp.float32))
        leaf_x[leaf] = value
    leave(leaf_x, leaf_out, out_sem.at[0])
    below, weights = jnp.concatenate(kept, axis=0), jnp.concatenate(reduced, axis=0)
    for level in range(3):
        if level > 0:
            pair_copy(level - 1, 1).wait_recv()
            pair_copy(level - 1, 2).wait_recv()
            below, weights = pair_z[level - 1], pair_r[level - 1]

        def keep(value):
            if level == 2:
                top_x[0] = value
            else:
                pair_z[level, pl.ds(pl.multiple_of(bits[level] * 64, 64), 64), :] = value
                pair_copy(level, 1).start()

        solved, _ = interpolate([below - exact(square[level], weights)], [picks[2 + level]], keep)
        value = exact(solved[0], weights)
        if level == 2:
            top_x[1] = value
            leave(top_x, top_out, out_sem.at[4])
        else:
            pair_r[level, pl.ds(pl.multiple_of(bits[level] * 64, 64), 64), :] = value
            pair_copy(level, 2).start()
        upper_x[level] = solved[0]
        leave(upper_x.at[level], upper_out.at[level], out_sem.at[1 + level])

    def drain(j, _):
        row_copy(j).wait_send()
        box_copy(j).wait_send()
        return 0

    lax.fori_loop(1, 16, drain, 0)
    for q in range(5):
        for dy in range(4):
            on_chip(dy, q).wait_send()
        upward(0, q).wait_send()
        downward(0, q).wait_send()
    for q in (4, 0, 1):
        upward(1, q).wait_send()
    for q in (2, 3):
        downward(3, q).wait_send()
    for level in range(2):
        for kind in range(3):
            pair_copy(level, kind).wait_send()
    pltpu.make_async_copy(leaf_x, leaf_out, out_sem.at[0]).wait()
    for level in range(3):
        pltpu.make_async_copy(upper_x.at[level], upper_out.at[level], out_sem.at[1 + level]).wait()
    pltpu.make_async_copy(top_x, top_out, out_sem.at[4]).wait()


def local(probes, points, leaf_skeleton, skeleton_one, skeleton_two, skeleton_three):
    bf16, f32, dma, vmem = jnp.bfloat16, jnp.float32, pltpu.SemaphoreType.DMA, pltpu.VMEM
    extent = OWN * lax.axis_size("row") * lax.axis_size("col")
    kernel_gain = 16.0 / math.sqrt(4 * extent)
    rows = 16 * OWN
    outside, inside = pl.BlockSpec(memory_space=pl.ANY), pl.BlockSpec(memory_space=vmem)
    leaf_interp, upper_interp, top_state = pl.pallas_call(
        partial(hss_kernel, kernel_gain),
        out_shape=(
            jax.ShapeDtypeStruct((2, 64, LEAF), f32),
            jax.ShapeDtypeStruct((3, 64, LEAF), f32),
            jax.ShapeDtypeStruct((2, 64, 256), f32),
        ),
        in_specs=[outside, inside, inside, inside, inside, inside],
        out_specs=(outside, outside, outside),
        scratch_shapes=[
            vmem((8 * CHUNK, 256), bf16),
            vmem((8, 4, 16, OWN), bf16),
            vmem((16, 16, OWN), bf16),
            vmem((FEATS, 8 * CHUNK), bf16),
            vmem((rows, FEATS), bf16),
            vmem((rows, 256), f32),
            vmem((16, OWN, 256), bf16),
            vmem((16, OWN, 256), bf16),
            vmem((5, 64, LEAF), bf16),
            vmem((3, LEAF, LEAF), f32),
            vmem((2, 2, 16, 64), bf16),
            vmem((2, LEAF, 256), f32),
            vmem((2, LEAF, 256), f32),
            vmem((2, 64, LEAF), f32),
            vmem((3, 64, LEAF), f32),
            vmem((2, 64, 256), f32),
            dma((4,)), dma((16,)), dma((16,)), dma((4, 5)), dma((2, 5)), dma((2, 5)), dma((8, 5)), dma((16,)), dma((16,)),
            dma((2, 3)), dma((2, 3)), dma((5,)),
        ],
        compiler_params=pltpu.CompilerParams(collective_id=0, has_side_effects=True, vmem_limit_bytes=60 << 20),
    )(probes, points, leaf_skeleton, skeleton_one, skeleton_two, skeleton_three)
    return leaf_interp.swapaxes(1, 2), upper_interp.swapaxes(1, 2)[:, None], top_state[:, None]


def solution(mesh):
    placed = (
        P(None, ("row", "col"), None),
        P(None, None, ("row", "col")),
        P(("row", "col"), None),
        P(("row", "col"), None),
        P("row", None),
        P("row", None),
    )
    return jax.shard_map(
        local,
        mesh=mesh,
        in_specs=placed,
        out_specs=(
            P(("row", "col"), None, None),
            P(None, ("row", "col"), None, None),
            P(None, ("row", "col"), None, None),
        ),
        check_vma=False,
    )
```

```python
import functools
import math

import jax
import jax.numpy as jnp
from jax import lax
from jax.experimental import pallas as pl
from jax.experimental.pallas import tpu as pltpu
from jax.sharding import PartitionSpec as P

LEAF = 128
MESH = pl.DeviceIdType.MESH
exact_mode = lax.Precision.HIGHEST
LOG2E = math.log2(math.e)
SIDE = 4
OWN = 256
CHUNK = 4 * OWN
FEATS = 64
PLACE = {(0, 0): 0, (0, 1): 1, (1, 0): 2, (3, 0): 3, (1, 1): 4, (3, 1): 5, (2, 0): 6, (2, 1): 7}
EARLY = 4
MIDWAY = 3


def pieces(value):
    high = value.astype(jnp.bfloat16).astype(jnp.float32)
    rest = value - high
    mid = rest.astype(jnp.bfloat16).astype(jnp.float32)
    return high, mid, rest - mid


def extra_rows(first, second, width=OWN):
    row = lax.broadcasted_iota(jnp.int32, (16, width), 0)
    out = jnp.zeros((16, width), jnp.float32)
    for i, value in enumerate((*first, *second)):
        out = jnp.where(row == i, value, out)
    return out


def exact(a, b, dims=((1,), (0,))):
    return lax.dot_general(a, b, (dims, ((), ())), precision=exact_mode, preferred_element_type=jnp.float32)

def split(v):
    h = v.astype(jnp.bfloat16)
    r = v - h.astype(jnp.float32)
    m = r.astype(jnp.bfloat16)
    return h, m, (r - m.astype(jnp.float32)).astype(jnp.bfloat16)

def select_rows(pick, values):
    return jnp.dot(jnp.concatenate([pick] * 3, axis=1), jnp.concatenate(split(values), axis=0), preferred_element_type=jnp.float32)

def pick_of(chosen):
    hits = lax.broadcasted_iota(jnp.int32, (128, 64), 0) == chosen
    return hits.astype(jnp.float32).T.astype(jnp.bfloat16)

def wide(col, width):
    return jnp.concatenate([col, col[:, :width - 128]], axis=1) if width > 128 else col[:, :width]

def eliminate(systems):
    width = systems[0].shape[1]
    sub = lax.broadcasted_iota(jnp.int32, (8, 1), 0)
    pivots = [m[0:8, :] for m in systems]
    systems = list(systems)
    for b in range(8):
        for s, m in enumerate(systems):
            p = pivots[s]
            lead = [jnp.broadcast_to(p[:, 8 * b + j:8 * b + j + 1], (8, 128)) for j in range(8)]
            for k in range(8):
                inv = 1.0 / lead[k][k:k + 1, :]
                f = lead[k] * inv
                q = p[k:k + 1, :]
                p = jnp.where(sub == k, q * wide(inv, width), p - wide(f, width) * q)
                for j in range(k + 1, 8):
                    q = lead[j][k:k + 1, :]
                    lead[j] = jnp.where(sub == k, q * inv, lead[j] - f * q)
            if b < 7:
                after = m[8 * b + 8:8 * b + 16, :]
                ahead = after
                for k in range(8):
                    ahead = ahead - wide(jnp.broadcast_to(after[:, 8 * b + k:8 * b + k + 1], (8, 128)), width) * p[k:k + 1, :]
                pivots[s] = ahead
            ch, cm, cl = split(m[:, 8 * b:8 * b + 8])
            ph, pm, low = split(p)
            change = jnp.dot(jnp.concatenate([ch, ch, cm, ch, cl, cm], axis=1), jnp.concatenate([ph, pm, ph, low, ph, pm], axis=0),
                             preferred_element_type=jnp.float32)
            rest = m - change
            systems[s] = jnp.concatenate(
                [p if i == b else pivots[s] if i == b + 1 else rest[8 * i:8 * i + 8, :] for i in range(8)], axis=0)
    return [m[:, 64:] for m in systems]


def interpolate(stacked, picks, keep=None):
    systems, kept = [], []
    eye = lax.broadcasted_iota(jnp.int32, (64, 64), 0) == lax.broadcasted_iota(jnp.int32, (64, 64), 1)
    for y, pick in zip(stacked, picks):
        z = select_rows(pick, y)
        kept.append(z)
        if keep is not None:
            keep(z)
        cross = exact(z, y, ((1,), (1,)))
        gram = lax.dot_general(jnp.concatenate(split(cross), axis=1), jnp.concatenate([pick] * 3, axis=1), (((1,), (1,)), ((), ())), preferred_element_type=jnp.float32)
        diag = jnp.where(eye, gram, 0.0)
        ridge = jnp.sum(diag, keepdims=True) * (0.05 / 64) + 1e-5
        gram = gram + jnp.where(eye, ridge, 0.0)
        systems.append(jnp.concatenate([gram, cross], axis=1))
    return eliminate(systems), kept


def kernel_square(gain, feats):
    sq = jnp.sum(feats * feats, axis=0, keepdims=True)
    ones = (jnp.ones((1, 128), jnp.float32),) * 3
    left = jnp.concatenate([*pieces(feats * (LOG2E / 16)), extra_rows(pieces(math.log2(gain) - sq * (LOG2E / 32)), ones, 128)], axis=0)
    right = jnp.concatenate([feats, feats, feats, extra_rows(ones, pieces(sq * (-LOG2E / 32)), 128)], axis=0)
    power = jnp.dot(left.T.astype(jnp.bfloat16), right.astype(jnp.bfloat16), preferred_element_type=jnp.float32)
    child = lax.broadcasted_iota(jnp.int32, (128, 128), 0) // 64
    other = lax.broadcasted_iota(jnp.int32, (128, 128), 1) // 64
    return jnp.where(child == other, 0.0, jnp.exp2(power))


def hss_kernel(gain, probes, points, chosen_leaf, chosen_one, chosen_two, chosen_three, leaf_out, upper_out, top_out,
               prb, pts, rpts, colf, rowf, acc, outbox, inbox, sum_out, sum_in, picks, square, pair_p, pair_z, pair_r, pair_out, pair_in, leaf_x, upper_x, top_x,
               loc_sem, rp_send, rp_recv, chip_send, up_send, down_send, got, box_send, box_recv, sum_send, sum_recv, pair_send, pair_recv, out_sem):
    row, col = lax.axis_index("row"), lax.axis_index("col")
    y, core = row // 2, lax.rem(row, 2)
    x, z = col // SIDE, lax.rem(col, SIDE)
    up = lax.rem(y + 1, SIDE) * 2 + core
    down = lax.rem(y + 3, SIDE) * 2 + core
    partner = y * 2 + 1 - core

    local = [pltpu.make_async_copy(probes.at[q], prb.at[pl.ds(q * OWN, OWN)], loc_sem.at[q]) for q in range(4)]
    for copy in local:
        copy.start()
    feats = points[...].astype(jnp.float32)
    for q in range(4):
        pts[0, q] = feats[:, q, :].astype(jnp.bfloat16)
    rpts[0] = pts[0, 0]

    def shifted(dx, dz):
        return lax.rem(x + dx + SIDE, SIDE) * SIDE + lax.rem(z + dz + SIDE, SIDE)

    def far(i):
        return 1 + i, 1 + lax.rem(i // 3 + 1, 3), 1 + lax.rem(i + 1, 3)

    def line(k, half):
        d = 1 + lax.rem(k + 1, 3)
        return (10 + 2 * k, 0, d) if half == 0 else (11 + 2 * k, d, 0)

    barrier = pltpu.get_barrier_semaphore()
    for other in (up, down, partner):
        pl.semaphore_signal(barrier, inc=1, device_id=(other, col), device_id_type=MESH)

    def each_peer(action):
        def on_axis(k, _):
            for half in range(2):
                action(*line(k, half))
            return 0

        def off_axis(i, _):
            action(*far(i))
            return 0

        lax.fori_loop(0, 3, on_axis, 0)
        lax.fori_loop(0, 9, off_axis, 0)

    def greet(slot, dx, dz):
        pl.semaphore_signal(barrier, inc=1, device_id=(row, shifted(dx, dz)), device_id_type=MESH)

    each_peer(greet)
    for copy in local:
        copy.wait()

    bits = (lax.rem(col, 2), lax.rem(col // 2, 2))

    def pair_copy(level, kind):
        bit = bits[level]
        if kind == 2:
            src_ref, dst_ref = pair_out.at[level], pair_in.at[level]
        else:
            src_ref = pair_p.at[level, bit] if kind == 0 else pair_z.at[level, pl.ds(pl.multiple_of(bit * 64, 64), 64)]
            dst_ref = src_ref
        return pltpu.make_async_remote_copy(
            src_ref=src_ref, dst_ref=dst_ref, send_sem=pair_send.at[level, kind], recv_sem=pair_recv.at[level, kind],
            device_id=(row, col + (1 - 2 * bit) * (level + 1)), device_id_type=MESH)

    for leaf in range(2):
        picks[leaf] = pick_of(chosen_leaf[leaf:leaf + 1, :])
    picks[2] = pick_of(chosen_one[...])
    picks[3] = pick_of(chosen_two[pl.ds(col // 2, 1), :])
    picks[4] = pick_of(chosen_three[pl.ds(col // 4, 1), :])

    def picked(feats, pick):
        return lax.dot_general(feats, pick, (((1,), (1,)), ((), ())), preferred_element_type=jnp.float32)

    def child_points(level, feats):
        square[level] = kernel_square(gain, feats)
        if level < 2:
            pair_p[level, bits[level]] = picked(feats.astype(jnp.bfloat16), picks[2 + level]).astype(jnp.bfloat16)

    def pair_points(level):
        pair_copy(level, 0).wait_recv()
        return jnp.concatenate([pair_p[level, 0], pair_p[level, 1]], axis=1).astype(jnp.float32)

    child_points(0, jnp.concatenate([picked(pts[0, 0, :, leaf * LEAF:(leaf + 1) * LEAF], picks[leaf]) for leaf in range(2)], axis=1))
    pl.semaphore_wait(barrier, 18)

    def row_copy(slot, dx, dz):
        return pltpu.make_async_remote_copy(
            src_ref=rpts.at[0], dst_ref=rpts.at[slot], send_sem=rp_send.at[slot], recv_sem=rp_recv.at[slot],
            device_id=(row, shifted(dx, dz)), device_id_type=MESH)

    def piece_copy(src, dst, q, sem, target):
        src_ref = pts.at[src] if q == 4 else prb.at[pl.ds(src * CHUNK + q * OWN, OWN)]
        dst_ref = pts.at[dst] if q == 4 else prb.at[pl.ds(dst * CHUNK + q * OWN, OWN)]
        return pltpu.make_async_remote_copy(
            src_ref=src_ref, dst_ref=dst_ref, send_sem=sem, recv_sem=got.at[dst, q],
            device_id=(target, col), device_id_type=MESH)

    def on_chip(dy, q):
        return piece_copy(PLACE[dy, 0], PLACE[dy, 1], q, chip_send.at[dy, q], partner)

    def upward(src_dy, q):
        return piece_copy(PLACE[src_dy, 0], PLACE[src_dy + 1, 0], q, up_send.at[src_dy, q], up)

    def downward(src_dy, q):
        return piece_copy(PLACE[src_dy, 0], PLACE[3 if src_dy == 0 else 2, 0], q, down_send.at[src_dy // 3, q], down)

    def arrived(dy, dc, q):
        place = PLACE[dy, dc]
        piece_copy(place, place, q, chip_send.at[0, 0], partner).wait_recv()

    on_chip(0, 4).start()
    upward(0, 4).start()
    downward(0, 4).start()
    each_peer(lambda slot, dx, dz: row_copy(slot, dx, dz).start())
    pair_copy(0, 0).start()
    for q in range(4):
        on_chip(0, q).start()
    for q, r in zip((0, 1, 2, 3), (2, 3, 0, 1)):
        upward(0, q).start()
        downward(0, r).start()

    def col_features(place):
        for q in range(4):
            feats = pts[place, q].astype(jnp.float32)
            bias = jnp.sum(feats * feats, axis=0, keepdims=True) * (-LOG2E / 32)
            ones = (jnp.float32(1),) * 3
            stacked = jnp.concatenate([feats, feats, feats, extra_rows(ones, pieces(bias))], axis=0)
            colf[:, pl.ds(place * CHUNK + q * OWN, OWN)] = stacked.astype(jnp.bfloat16)

    def row_features(j):
        feats = rpts[j].astype(jnp.float32)
        bias = math.log2(gain) - jnp.sum(feats * feats, axis=0, keepdims=True) * (LOG2E / 32)
        ones = (jnp.float32(1),) * 3
        stacked = jnp.concatenate([*pieces(feats * (LOG2E / 16)), extra_rows(pieces(bias), ones)], axis=0)
        rowf[pl.ds(pl.multiple_of(j * OWN, OWN), OWN), :] = stacked.T.astype(jnp.bfloat16)

    def at(slot, count):
        return pl.ds(pl.multiple_of(slot * OWN, OWN), count * OWN)

    def partial(slot, count, first, last):
        cols = pl.ds(first * CHUNK, (last - first) * CHUNK)
        power = jnp.dot(rowf[at(slot, count), :], colf[:, cols], preferred_element_type=jnp.float32)
        return jnp.dot(jnp.exp2(power).astype(jnp.bfloat16), prb[cols, :], preferred_element_type=jnp.float32)

    col_features(0)
    row_features(0)
    power = jnp.dot(rowf[pl.ds(0, OWN), :], colf[:, pl.ds(0, CHUNK)], preferred_element_type=jnp.float32)
    leaf_of = lax.broadcasted_iota(jnp.int32, (OWN, CHUNK), 0) // LEAF
    other_leaf = lax.broadcasted_iota(jnp.int32, (OWN, CHUNK), 1) // LEAF
    tile = jnp.where(leaf_of == other_leaf, 0.0, jnp.exp2(power)).astype(jnp.bfloat16)
    own_sum = jnp.dot(tile, prb[pl.ds(0, CHUNK), :], preferred_element_type=jnp.float32)
    for q in (4, 0, 1, 2, 3):
        arrived(0, 1, q)
    col_features(1)
    acc[at(0, 1), :] = own_sum + partial(0, 1, 1, 2)

    def near_line(k, _):
        for half in range(2):
            slot, dx, dz = line(k, half)
            row_copy(slot, dx, dz).wait_recv()
            row_features(slot)
        acc[at(10 + 2 * k, 2), :] = partial(10 + 2 * k, 2, 0, 2)
        return 0

    def near_far(i, _):
        for e in range(3):
            slot, dx, dz = far(3 * i + e)
            row_copy(slot, dx, dz).wait_recv()
            row_features(slot)
        acc[at(1 + 3 * i, 3), :] = partial(1 + 3 * i, 3, 0, 2)
        return 0

    lax.fori_loop(0, 3, near_line, 0)
    for q in (4, 0, 1):
        arrived(1, 0, q)
        upward(1, q).start()
        on_chip(1, q).start()
    for q in (4, 2, 3):
        arrived(3, 0, q)
        if q != 4:
            downward(3, q).start()
        on_chip(3, q).start()
    lax.fori_loop(0, 3, near_far, 0)
    for q, r in ((2, 0), (3, 1)):
        arrived(1, 0, q)
        on_chip(1, q).start()
        arrived(3, 0, r)
        on_chip(3, r).start()
    for place in range(2, EARLY):
        col_features(place)
    child_points(1, pair_points(0))
    pair_copy(1, 0).start()

    def middle(i, _):
        @pl.when(i == MIDWAY)
        def _():
            for q in (4, 0, 2, 1, 3):
                arrived(2, 0, q)
                on_chip(2, q).start()

        acc[at(4 * i, 4), :] += partial(4 * i, 4, 2, EARLY)
        return 0

    lax.fori_loop(0, 4, middle, 0)
    child_points(2, pair_points(1))
    for dy in (1, 3, 2):
        for q in (4, 0, 1, 2, 3):
            arrived(dy, 1, q)
    for place in range(EARLY, 8):
        col_features(place)

    def box_copy(half, slot, dx, dz):
        target = shifted(-dx, 0) if half == 0 else shifted(0, -dz)
        return pltpu.make_async_remote_copy(
            src_ref=outbox.at[slot, half], dst_ref=inbox.at[half, slot],
            send_sem=box_send.at[half, slot], recv_sem=box_recv.at[half, slot],
            device_id=(row, target), device_id_type=MESH)

    def sum_copy(half, k):
        _, dx, dz = line(k, half)
        return pltpu.make_async_remote_copy(
            src_ref=sum_out.at[half, k], dst_ref=sum_in.at[half, k], send_sem=sum_send.at[half, k], recv_sem=sum_recv.at[half, k],
            device_id=(row, shifted(-dx, -dz)), device_id_type=MESH)

    def half_of(value, half):
        return value[:, half * 128:(half + 1) * 128]

    def far_blocks(i, _):
        total = acc[at(1 + 3 * i, 3), :] + partial(1 + 3 * i, 3, EARLY, 8)
        for e in range(3):
            slot, dx, dz = far(3 * i + e)
            for half in range(2):
                outbox[slot, half] = half_of(total[e * OWN:(e + 1) * OWN], half).astype(jnp.bfloat16)
                box_copy(half, slot, dx, dz).start()
        return 0

    def line_blocks(k, _):
        total = acc[at(10 + 2 * k, 2), :] + partial(10 + 2 * k, 2, EARLY, 8)
        for half in range(2):
            slot, dx, dz = line(k, half)
            mine, other = total[half * OWN:(half + 1) * OWN], 1 - half
            outbox[slot, other] = half_of(mine, other).astype(jnp.bfloat16)
            box_copy(other, slot, dx, dz).start()
            summed = half_of(mine, half)
            for e in range(3):
                source, dx, dz = far(3 * e + k if half == 0 else 3 * k + e)
                box_copy(half, source, dx, dz).wait_recv()
                summed = summed + inbox[half, source].astype(jnp.float32)
            sum_out[half, k] = summed
            sum_copy(half, k).start()
        return 0

    lax.fori_loop(0, 3, far_blocks, 0)
    lax.fori_loop(0, 3, line_blocks, 0)
    total = acc[at(0, 1), :] + partial(0, 1, EARLY, 8)
    for half in range(2):
        summed = half_of(total, half)
        for k in range(3):
            slot, dx, dz = line(k, 1 - half)
            box_copy(half, slot, dx, dz).wait_recv()
            summed = summed + inbox[half, slot].astype(jnp.float32)
            sum_copy(half, k).wait_recv()
            summed = summed + sum_in[half, k]
        acc[pl.ds(0, OWN), half * 128:(half + 1) * 128] = summed

    def leave(src, dst, sem):
        pltpu.make_async_copy(src, dst, sem).start()

    solved, kept = interpolate([acc[pl.ds(leaf * LEAF, LEAF), :] for leaf in range(2)], [picks[0], picks[1]])
    reduced = []
    for leaf, value in enumerate(solved):
        rows = prb[pl.ds(leaf * LEAF, LEAF), :]
        reduced.append(jnp.dot(jnp.concatenate(split(value), axis=1), jnp.concatenate([rows] * 3, axis=0), preferred_element_type=jnp.float32))
        leaf_x[leaf] = value
    leave(leaf_x, leaf_out, out_sem.at[0])
    below, weights = jnp.concatenate(kept, axis=0), jnp.concatenate(reduced, axis=0)
    for level in range(3):
        if level > 0:
            pair_copy(level - 1, 1).wait_recv()
            pair_copy(level - 1, 2).wait_recv()
            pair_r[level - 1, pl.ds(pl.multiple_of(64 - bits[level - 1] * 64, 64), 64), :] = pair_in[level - 1].astype(jnp.float32)
            below, weights = pair_z[level - 1], pair_r[level - 1]

        def keep(value):
            if level == 2:
                top_x[0] = value
            else:
                pair_z[level, pl.ds(pl.multiple_of(bits[level] * 64, 64), 64), :] = value
                pair_copy(level, 1).start()

        solved, _ = interpolate([below - exact(square[level], weights)], [picks[2 + level]], keep)
        value = exact(solved[0], weights)
        if level == 2:
            top_x[1] = value
            leave(top_x, top_out, out_sem.at[4])
        else:
            pair_out[level] = value.astype(jnp.bfloat16)
            pair_copy(level, 2).start()
            pair_r[level, pl.ds(pl.multiple_of(bits[level] * 64, 64), 64), :] = value
        upper_x[level] = solved[0]
        leave(upper_x.at[level], upper_out.at[level], out_sem.at[1 + level])

    def drain(slot, dx, dz):
        row_copy(slot, dx, dz).wait_send()

    each_peer(drain)

    def drain_far(i, _):
        for half in range(2):
            box_copy(half, *far(i)).wait_send()
        return 0

    lax.fori_loop(0, 9, drain_far, 0)
    for k in range(3):
        for half in range(2):
            box_copy(half, *line(k, 1 - half)).wait_send()
            sum_copy(half, k).wait_send()
    for q in range(5):
        for dy in range(4):
            on_chip(dy, q).wait_send()
        upward(0, q).wait_send()
        downward(0, q).wait_send()
    for q in (4, 0, 1):
        upward(1, q).wait_send()
    for q in (2, 3):
        downward(3, q).wait_send()
    for level in range(2):
        for kind in range(3):
            pair_copy(level, kind).wait_send()
    pltpu.make_async_copy(leaf_x, leaf_out, out_sem.at[0]).wait()
    for level in range(3):
        pltpu.make_async_copy(upper_x.at[level], upper_out.at[level], out_sem.at[1 + level]).wait()
    pltpu.make_async_copy(top_x, top_out, out_sem.at[4]).wait()


def local(probes, points, leaf_skeleton, skeleton_one, skeleton_two, skeleton_three):
    bf16, f32, dma, vmem = jnp.bfloat16, jnp.float32, pltpu.SemaphoreType.DMA, pltpu.VMEM
    extent = OWN * lax.axis_size("row") * lax.axis_size("col")
    kernel_gain = 16.0 / math.sqrt(4 * extent)
    rows = 16 * OWN
    outside, inside = pl.BlockSpec(memory_space=pl.ANY), pl.BlockSpec(memory_space=vmem)
    leaf_interp, upper_interp, top_state = pl.pallas_call(
        functools.partial(hss_kernel, kernel_gain),
        out_shape=(
            jax.ShapeDtypeStruct((2, 64, LEAF), f32),
            jax.ShapeDtypeStruct((3, 64, LEAF), f32),
            jax.ShapeDtypeStruct((2, 64, 256), f32),
        ),
        in_specs=[outside, inside, inside, inside, inside, inside],
        out_specs=(outside, outside, outside),
        scratch_shapes=[
            vmem((8 * CHUNK, 256), bf16),
            vmem((8, 4, 16, OWN), bf16),
            vmem((16, 16, OWN), bf16),
            vmem((FEATS, 8 * CHUNK), bf16),
            vmem((rows, FEATS), bf16),
            vmem((rows, 256), f32),
            vmem((16, 2, OWN, 128), bf16),
            vmem((2, 16, OWN, 128), bf16),
            vmem((2, 3, OWN, 128), f32),
            vmem((2, 3, OWN, 128), f32),
            vmem((5, 64, LEAF), bf16),
            vmem((3, LEAF, LEAF), f32),
            vmem((2, 2, 16, 64), bf16),
            vmem((2, LEAF, 256), f32),
            vmem((2, LEAF, 256), f32),
            vmem((2, 64, 256), bf16),
            vmem((2, 64, 256), bf16),
            vmem((2, 64, LEAF), f32),
            vmem((3, 64, LEAF), f32),
            vmem((2, 64, 256), f32),
            dma((4,)), dma((16,)), dma((16,)), dma((4, 5)), dma((2, 5)), dma((2, 5)), dma((8, 5)), dma((2, 16)), dma((2, 16)), dma((2, 3)), dma((2, 3)),
            dma((2, 3)), dma((2, 3)), dma((5,)),
        ],
        compiler_params=pltpu.CompilerParams(collective_id=0, has_side_effects=True, vmem_limit_bytes=60 << 20),
    )(probes, points, leaf_skeleton, skeleton_one, skeleton_two, skeleton_three)
    return leaf_interp.swapaxes(1, 2), upper_interp.swapaxes(1, 2)[:, None], top_state[:, None]


def solution(mesh):
    placed = (
        P(None, ("row", "col"), None),
        P(None, None, ("row", "col")),
        P(("row", "col"), None),
        P(("row", "col"), None),
        P("row", None),
        P("row", None),
    )
    return jax.shard_map(
        local,
        mesh=mesh,
        in_specs=placed,
        out_specs=(
            P(("row", "col"), None, None),
            P(None, ("row", "col"), None, None),
            P(None, ("row", "col"), None, None),
        ),
        check_vma=False,
    )
```

```python
import functools
import math

import jax
import jax.numpy as jnp
from jax import lax
from jax.experimental import pallas as pl
from jax.experimental.pallas import tpu as pltpu
from jax.sharding import PartitionSpec as P

LEAF = 128
MESH = pl.DeviceIdType.MESH
exact_mode = lax.Precision.HIGHEST
LOG2E = math.log2(math.e)
SIDE = 4
OWN = 256
CHUNK = 4 * OWN
FEATS = 64
PLACE = {(0, 0): 0, (0, 1): 1, (1, 0): 2, (3, 0): 3, (1, 1): 4, (3, 1): 5, (2, 0): 6, (2, 1): 7}
EARLY = 4
MIDWAY = 3


def pieces(value):
    high = value.astype(jnp.bfloat16).astype(jnp.float32)
    rest = value - high
    mid = rest.astype(jnp.bfloat16).astype(jnp.float32)
    return high, mid, rest - mid


def extra_rows(first, second, width=OWN):
    row = lax.broadcasted_iota(jnp.int32, (16, width), 0)
    out = jnp.zeros((16, width), jnp.float32)
    for i, value in enumerate((*first, *second)):
        out = jnp.where(row == i, value, out)
    return out


def exact(a, b, dims=((1,), (0,))):
    return lax.dot_general(a, b, (dims, ((), ())), precision=exact_mode, preferred_element_type=jnp.float32)

def split(v):
    h = v.astype(jnp.bfloat16)
    r = v - h.astype(jnp.float32)
    m = r.astype(jnp.bfloat16)
    return h, m, (r - m.astype(jnp.float32)).astype(jnp.bfloat16)

def select_rows(pick, values):
    return jnp.dot(jnp.concatenate([pick] * 3, axis=1), jnp.concatenate(split(values), axis=0), preferred_element_type=jnp.float32)

def pick_of(chosen):
    hits = lax.broadcasted_iota(jnp.int32, (128, 64), 0) == chosen
    return hits.astype(jnp.float32).T.astype(jnp.bfloat16)

def wide(col, width):
    return jnp.concatenate([col, col[:, :width - 128]], axis=1) if width > 128 else col[:, :width]

def eliminate(systems):
    width = systems[0].shape[1]
    sub = lax.broadcasted_iota(jnp.int32, (8, 1), 0)
    pivots = [m[0:8, :] for m in systems]
    systems = list(systems)
    for b in range(8):
        for s, m in enumerate(systems):
            p = pivots[s]
            lead = [jnp.broadcast_to(p[:, 8 * b + j:8 * b + j + 1], (8, 128)) for j in range(8)]
            for k in range(8):
                inv = 1.0 / lead[k][k:k + 1, :]
                f = lead[k] * inv
                q = p[k:k + 1, :]
                p = jnp.where(sub == k, q * wide(inv, width), p - wide(f, width) * q)
                for j in range(k + 1, 8):
                    q = lead[j][k:k + 1, :]
                    lead[j] = jnp.where(sub == k, q * inv, lead[j] - f * q)
            if b < 7:
                after = m[8 * b + 8:8 * b + 16, :]
                ahead = after
                for k in range(8):
                    ahead = ahead - wide(jnp.broadcast_to(after[:, 8 * b + k:8 * b + k + 1], (8, 128)), width) * p[k:k + 1, :]
                pivots[s] = ahead
            ch, cm, cl = split(m[:, 8 * b:8 * b + 8])
            ph, pm, low = split(p)
            change = jnp.dot(jnp.concatenate([ch, ch, cm, ch, cl, cm], axis=1), jnp.concatenate([ph, pm, ph, low, ph, pm], axis=0),
                             preferred_element_type=jnp.float32)
            rest = m - change
            systems[s] = jnp.concatenate(
                [p if i == b else pivots[s] if i == b + 1 else rest[8 * i:8 * i + 8, :] for i in range(8)], axis=0)
    return [m[:, 64:] for m in systems]


def interpolate(stacked, picks, keep=None):
    systems, kept = [], []
    eye = lax.broadcasted_iota(jnp.int32, (64, 64), 0) == lax.broadcasted_iota(jnp.int32, (64, 64), 1)
    for y, pick in zip(stacked, picks):
        z = select_rows(pick, y)
        kept.append(z)
        if keep is not None:
            keep(z)
        cross = exact(z, y, ((1,), (1,)))
        gram = lax.dot_general(jnp.concatenate(split(cross), axis=1), jnp.concatenate([pick] * 3, axis=1), (((1,), (1,)), ((), ())), preferred_element_type=jnp.float32)
        diag = jnp.where(eye, gram, 0.0)
        ridge = jnp.sum(diag, keepdims=True) * (0.05 / 64) + 1e-5
        gram = gram + jnp.where(eye, ridge, 0.0)
        systems.append(jnp.concatenate([gram, cross], axis=1))
    return eliminate(systems), kept


def kernel_square(gain, feats):
    sq = jnp.sum(feats * feats, axis=0, keepdims=True)
    ones = (jnp.ones((1, 128), jnp.float32),) * 3
    left = jnp.concatenate([*pieces(feats * (LOG2E / 16)), extra_rows(pieces(math.log2(gain) - sq * (LOG2E / 32)), ones, 128)], axis=0)
    right = jnp.concatenate([feats, feats, feats, extra_rows(ones, pieces(sq * (-LOG2E / 32)), 128)], axis=0)
    power = jnp.dot(left.T.astype(jnp.bfloat16), right.astype(jnp.bfloat16), preferred_element_type=jnp.float32)
    child = lax.broadcasted_iota(jnp.int32, (128, 128), 0) // 64
    other = lax.broadcasted_iota(jnp.int32, (128, 128), 1) // 64
    return jnp.where(child == other, 0.0, jnp.exp2(power))


def hss_kernel(gain, probes, points, table_leaf, table_one, table_two, table_three, leaf_out, upper_out, top_out,
               raw, chosen_leaf, chosen_one, chosen_two, chosen_three, prb, pts, rpts, colf, rowf, acc, outbox, inbox, sum_out, sum_in, picks, square, pair_p, pair_z, pair_r, pair_out, pair_in, leaf_x, upper_x, top_x,
               loc_sem, rp_send, rp_recv, chip_send, up_send, down_send, got, box_send, box_recv, sum_send, sum_recv, pair_send, pair_recv, out_sem):
    tables = (table_leaf, table_one, table_two, table_three)
    row, col = lax.axis_index("row"), lax.axis_index("col")
    y, core = row // 2, lax.rem(row, 2)
    x, z = col // SIDE, lax.rem(col, SIDE)
    up = lax.rem(y + 1, SIDE) * 2 + core
    down = lax.rem(y + 3, SIDE) * 2 + core
    partner = y * 2 + 1 - core

    def shifted(dx, dz):
        return lax.rem(x + dx + SIDE, SIDE) * SIDE + lax.rem(z + dz + SIDE, SIDE)

    def far(i):
        return 1 + i, 1 + lax.rem(i // 3 + 1, 3), 1 + lax.rem(i + 1, 3)

    def line(k, half):
        d = 1 + lax.rem(k + 1, 3)
        return (10 + 2 * k, 0, d) if half == 0 else (11 + 2 * k, d, 0)

    barrier = pltpu.get_barrier_semaphore()
    for other in (up, down, partner):
        pl.semaphore_signal(barrier, inc=1, device_id=(other, col), device_id_type=MESH)

    def each_peer(action):
        def on_axis(k, _):
            for half in range(2):
                action(*line(k, half))
            return 0

        def off_axis(i, _):
            action(*far(i))
            return 0

        lax.fori_loop(0, 3, on_axis, 0)
        lax.fori_loop(0, 9, off_axis, 0)

    def greet(slot, dx, dz):
        pl.semaphore_signal(barrier, inc=1, device_id=(row, shifted(dx, dz)), device_id_type=MESH)

    each_peer(greet)
    local = [pltpu.make_async_copy(points, raw, loc_sem.at[4])]
    local += [pltpu.make_async_copy(probes.at[q], prb.at[pl.ds(q * OWN, OWN)], loc_sem.at[q]) for q in range(4)]
    for i, (src, dst) in enumerate(zip(tables, (chosen_leaf, chosen_one, chosen_two, chosen_three))):
        local.append(pltpu.make_async_copy(src, dst, loc_sem.at[5 + i]))
    for copy in local:
        copy.start()
    local[0].wait()
    feats = raw[...].astype(jnp.float32)
    for q in range(4):
        pts[0, q] = feats[:, q, :].astype(jnp.bfloat16)
    rpts[0] = pts[0, 0]
    for copy in local[1:]:
        copy.wait()

    bits = (lax.rem(col, 2), lax.rem(col // 2, 2))

    def pair_copy(level, kind):
        bit = bits[level]
        if kind == 2:
            src_ref, dst_ref = pair_out.at[level], pair_in.at[level]
        else:
            src_ref = pair_p.at[level, bit] if kind == 0 else pair_z.at[level, pl.ds(pl.multiple_of(bit * 64, 64), 64)]
            dst_ref = src_ref
        return pltpu.make_async_remote_copy(
            src_ref=src_ref, dst_ref=dst_ref, send_sem=pair_send.at[level, kind], recv_sem=pair_recv.at[level, kind],
            device_id=(row, col + (1 - 2 * bit) * (level + 1)), device_id_type=MESH)

    pl.semaphore_wait(barrier, 18)

    def row_copy(slot, dx, dz):
        return pltpu.make_async_remote_copy(
            src_ref=rpts.at[0], dst_ref=rpts.at[slot], send_sem=rp_send.at[slot], recv_sem=rp_recv.at[slot],
            device_id=(row, shifted(dx, dz)), device_id_type=MESH)

    def piece_copy(src, dst, q, sem, target):
        src_ref = pts.at[src] if q == 4 else prb.at[pl.ds(src * CHUNK + q * OWN, OWN)]
        dst_ref = pts.at[dst] if q == 4 else prb.at[pl.ds(dst * CHUNK + q * OWN, OWN)]
        return pltpu.make_async_remote_copy(
            src_ref=src_ref, dst_ref=dst_ref, send_sem=sem, recv_sem=got.at[dst, q],
            device_id=(target, col), device_id_type=MESH)

    def on_chip(dy, q):
        return piece_copy(PLACE[dy, 0], PLACE[dy, 1], q, chip_send.at[dy, q], partner)

    def upward(src_dy, q):
        return piece_copy(PLACE[src_dy, 0], PLACE[src_dy + 1, 0], q, up_send.at[src_dy, q], up)

    def downward(src_dy, q):
        return piece_copy(PLACE[src_dy, 0], PLACE[3 if src_dy == 0 else 2, 0], q, down_send.at[src_dy // 3, q], down)

    def arrived(dy, dc, q):
        place = PLACE[dy, dc]
        piece_copy(place, place, q, chip_send.at[0, 0], partner).wait_recv()

    on_chip(0, 4).start()
    upward(0, 4).start()
    downward(0, 4).start()
    each_peer(lambda slot, dx, dz: row_copy(slot, dx, dz).start())
    for q in range(4):
        on_chip(0, q).start()
    for q, r in zip((0, 1, 2, 3), (2, 3, 0, 1)):
        upward(0, q).start()
        downward(0, r).start()

    for leaf in range(2):
        picks[leaf] = pick_of(chosen_leaf[leaf:leaf + 1, :])
    picks[2] = pick_of(chosen_one[...])
    picks[3] = pick_of(chosen_two[pl.ds(col // 2, 1), :])
    picks[4] = pick_of(chosen_three[pl.ds(col // 4, 1), :])

    def picked(feats, pick):
        return lax.dot_general(feats, pick, (((1,), (1,)), ((), ())), preferred_element_type=jnp.float32)

    def child_points(level, feats):
        square[level] = kernel_square(gain, feats)
        if level < 2:
            pair_p[level, bits[level]] = picked(feats.astype(jnp.bfloat16), picks[2 + level]).astype(jnp.bfloat16)

    def pair_points(level):
        pair_copy(level, 0).wait_recv()
        return jnp.concatenate([pair_p[level, 0], pair_p[level, 1]], axis=1).astype(jnp.float32)

    child_points(0, jnp.concatenate([picked(pts[0, 0, :, leaf * LEAF:(leaf + 1) * LEAF], picks[leaf]) for leaf in range(2)], axis=1))
    pair_copy(0, 0).start()

    def col_features(place):
        for q in range(4):
            feats = pts[place, q].astype(jnp.float32)
            bias = jnp.sum(feats * feats, axis=0, keepdims=True) * (-LOG2E / 32)
            ones = (jnp.float32(1),) * 3
            stacked = jnp.concatenate([feats, feats, feats, extra_rows(ones, pieces(bias))], axis=0)
            colf[:, pl.ds(place * CHUNK + q * OWN, OWN)] = stacked.astype(jnp.bfloat16)

    def row_features(j):
        feats = rpts[j].astype(jnp.float32)
        bias = math.log2(gain) - jnp.sum(feats * feats, axis=0, keepdims=True) * (LOG2E / 32)
        ones = (jnp.float32(1),) * 3
        stacked = jnp.concatenate([*pieces(feats * (LOG2E / 16)), extra_rows(pieces(bias), ones)], axis=0)
        rowf[pl.ds(pl.multiple_of(j * OWN, OWN), OWN), :] = stacked.T.astype(jnp.bfloat16)

    def at(slot, count):
        return pl.ds(pl.multiple_of(slot * OWN, OWN), count * OWN)

    def partial(slot, count, first, last):
        cols = pl.ds(first * CHUNK, (last - first) * CHUNK)
        power = jnp.dot(rowf[at(slot, count), :], colf[:, cols], preferred_element_type=jnp.float32)
        return jnp.dot(jnp.exp2(power).astype(jnp.bfloat16), prb[cols, :], preferred_element_type=jnp.float32)

    col_features(0)
    row_features(0)
    power = jnp.dot(rowf[pl.ds(0, OWN), :], colf[:, pl.ds(0, CHUNK)], preferred_element_type=jnp.float32)
    leaf_of = lax.broadcasted_iota(jnp.int32, (OWN, CHUNK), 0) // LEAF
    other_leaf = lax.broadcasted_iota(jnp.int32, (OWN, CHUNK), 1) // LEAF
    tile = jnp.where(leaf_of == other_leaf, 0.0, jnp.exp2(power)).astype(jnp.bfloat16)
    own_sum = jnp.dot(tile, prb[pl.ds(0, CHUNK), :], preferred_element_type=jnp.float32)
    for q in (4, 0, 1, 2, 3):
        arrived(0, 1, q)
    col_features(1)
    acc[at(0, 1), :] = own_sum + partial(0, 1, 1, 2)

    def near_line(k, _):
        for half in range(2):
            slot, dx, dz = line(k, half)
            row_copy(slot, dx, dz).wait_recv()
            row_features(slot)
        acc[at(10 + 2 * k, 2), :] = partial(10 + 2 * k, 2, 0, 2)
        return 0

    def near_far(i, _):
        for e in range(3):
            slot, dx, dz = far(3 * i + e)
            row_copy(slot, dx, dz).wait_recv()
            row_features(slot)
        acc[at(1 + 3 * i, 3), :] = partial(1 + 3 * i, 3, 0, 2)
        return 0

    lax.fori_loop(0, 3, near_line, 0)
    for q in (4, 0, 1):
        arrived(1, 0, q)
        upward(1, q).start()
        on_chip(1, q).start()
    for q in (4, 2, 3):
        arrived(3, 0, q)
        if q != 4:
            downward(3, q).start()
        on_chip(3, q).start()
    lax.fori_loop(0, 3, near_far, 0)
    for q, r in ((2, 0), (3, 1)):
        arrived(1, 0, q)
        on_chip(1, q).start()
        arrived(3, 0, r)
        on_chip(3, r).start()
    for place in range(2, EARLY):
        col_features(place)
    child_points(1, pair_points(0))
    pair_copy(1, 0).start()

    def middle(i, _):
        @pl.when(i == MIDWAY)
        def _():
            for q in (4, 0, 2, 1, 3):
                arrived(2, 0, q)
                on_chip(2, q).start()

        acc[at(1 + 3 * i, 3), :] += partial(1 + 3 * i, 3, 2, EARLY)
        return 0

    lax.fori_loop(0, 5, middle, 0)
    child_points(2, pair_points(1))
    for dy in (1, 3, 2):
        for q in (4, 0, 1, 2, 3):
            arrived(dy, 1, q)
    for place in range(EARLY, 8):
        col_features(place)

    def box_copy(half, slot, dx, dz):
        target = shifted(-dx, 0) if half == 0 else shifted(0, -dz)
        return pltpu.make_async_remote_copy(
            src_ref=outbox.at[slot, half], dst_ref=inbox.at[half, slot],
            send_sem=box_send.at[half, slot], recv_sem=box_recv.at[half, slot],
            device_id=(row, target), device_id_type=MESH)

    def sum_copy(half, k):
        _, dx, dz = line(k, half)
        return pltpu.make_async_remote_copy(
            src_ref=sum_out.at[half, k], dst_ref=sum_in.at[half, k], send_sem=sum_send.at[half, k], recv_sem=sum_recv.at[half, k],
            device_id=(row, shifted(-dx, -dz)), device_id_type=MESH)

    def half_of(value, half):
        return value[:, half * 128:(half + 1) * 128]

    def far_blocks(i, _):
        total = acc[at(1 + 3 * i, 3), :] + partial(1 + 3 * i, 3, EARLY, 8)
        for e in range(3):
            slot, dx, dz = far(3 * i + e)
            for half in range(2):
                outbox[slot, half] = half_of(total[e * OWN:(e + 1) * OWN], half).astype(jnp.bfloat16)
                box_copy(half, slot, dx, dz).start()
        return 0

    def line_blocks(k, _):
        total = acc[at(10 + 2 * k, 2), :] + partial(10 + 2 * k, 2, EARLY, 8)
        for half in range(2):
            slot, dx, dz = line(k, half)
            mine, other = total[half * OWN:(half + 1) * OWN], 1 - half
            outbox[slot, other] = half_of(mine, other).astype(jnp.bfloat16)
            box_copy(other, slot, dx, dz).start()
            summed = half_of(mine, half)
            for e in range(3):
                source, dx, dz = far(3 * e + k if half == 0 else 3 * k + e)
                box_copy(half, source, dx, dz).wait_recv()
                summed = summed + inbox[half, source].astype(jnp.float32)
            sum_out[half, k] = summed
            sum_copy(half, k).start()
        return 0

    lax.fori_loop(0, 3, far_blocks, 0)
    lax.fori_loop(0, 3, line_blocks, 0)
    total = acc[at(0, 1), :] + partial(0, 1, 2, 8)
    for half in range(2):
        summed = half_of(total, half)
        for k in range(3):
            slot, dx, dz = line(k, 1 - half)
            box_copy(half, slot, dx, dz).wait_recv()
            summed = summed + inbox[half, slot].astype(jnp.float32)
            sum_copy(half, k).wait_recv()
            summed = summed + sum_in[half, k]
        acc[pl.ds(0, OWN), half * 128:(half + 1) * 128] = summed

    def leave(src, dst, sem):
        pltpu.make_async_copy(src, dst, sem).start()

    solved, kept = interpolate([acc[pl.ds(leaf * LEAF, LEAF), :] for leaf in range(2)], [picks[0], picks[1]])
    reduced = []
    for leaf, value in enumerate(solved):
        rows = prb[pl.ds(leaf * LEAF, LEAF), :]
        reduced.append(jnp.dot(jnp.concatenate(split(value), axis=1), jnp.concatenate([rows] * 3, axis=0), preferred_element_type=jnp.float32))
        leaf_x[leaf] = value
    leave(leaf_x, leaf_out, out_sem.at[0])
    below, weights = jnp.concatenate(kept, axis=0), jnp.concatenate(reduced, axis=0)
    for level in range(3):
        if level > 0:
            pair_copy(level - 1, 1).wait_recv()
            pair_copy(level - 1, 2).wait_recv()
            pair_r[level - 1, pl.ds(pl.multiple_of(64 - bits[level - 1] * 64, 64), 64), :] = pair_in[level - 1].astype(jnp.float32)
            below, weights = pair_z[level - 1], pair_r[level - 1]

        def keep(value):
            if level == 2:
                top_x[0] = value
            else:
                pair_z[level, pl.ds(pl.multiple_of(bits[level] * 64, 64), 64), :] = value
                pair_copy(level, 1).start()

        solved, _ = interpolate([below - exact(square[level], weights)], [picks[2 + level]], keep)
        value = exact(solved[0], weights)
        if level == 2:
            top_x[1] = value
            leave(top_x, top_out, out_sem.at[4])
        else:
            pair_out[level] = value.astype(jnp.bfloat16)
            pair_copy(level, 2).start()
            pair_r[level, pl.ds(pl.multiple_of(bits[level] * 64, 64), 64), :] = value
        upper_x[level] = solved[0]
        leave(upper_x.at[level], upper_out.at[level], out_sem.at[1 + level])

    def drain(slot, dx, dz):
        row_copy(slot, dx, dz).wait_send()

    each_peer(drain)

    def drain_far(i, _):
        for half in range(2):
            box_copy(half, *far(i)).wait_send()
        return 0

    lax.fori_loop(0, 9, drain_far, 0)
    for k in range(3):
        for half in range(2):
            box_copy(half, *line(k, 1 - half)).wait_send()
            sum_copy(half, k).wait_send()
    for q in range(5):
        for dy in range(4):
            on_chip(dy, q).wait_send()
        upward(0, q).wait_send()
        downward(0, q).wait_send()
    for q in (4, 0, 1):
        upward(1, q).wait_send()
    for q in (2, 3):
        downward(3, q).wait_send()
    for level in range(2):
        for kind in range(3):
            pair_copy(level, kind).wait_send()
    pltpu.make_async_copy(leaf_x, leaf_out, out_sem.at[0]).wait()
    for level in range(3):
        pltpu.make_async_copy(upper_x.at[level], upper_out.at[level], out_sem.at[1 + level]).wait()
    pltpu.make_async_copy(top_x, top_out, out_sem.at[4]).wait()


def finish_kernel(leaf, upper, top, leaf_out, upper_out, top_out):
    leaf_out[...] = leaf[...]
    upper_out[...] = upper[...]
    top_out[...] = top[...]


def local(probes, points, leaf_skeleton, skeleton_one, skeleton_two, skeleton_three):
    bf16, f32, dma, vmem = jnp.bfloat16, jnp.float32, pltpu.SemaphoreType.DMA, pltpu.VMEM
    extent = OWN * lax.axis_size("row") * lax.axis_size("col")
    kernel_gain = 16.0 / math.sqrt(4 * extent)
    rows = 16 * OWN
    outside, inside = pl.BlockSpec(memory_space=pl.ANY), pl.BlockSpec(memory_space=vmem)
    outputs = (
        jax.ShapeDtypeStruct((2, 64, LEAF), f32),
        jax.ShapeDtypeStruct((3, 64, LEAF), f32),
        jax.ShapeDtypeStruct((2, 64, 256), f32),
    )
    results = pl.pallas_call(
        functools.partial(hss_kernel, kernel_gain),
        out_shape=outputs,
        in_specs=[outside] * 6,
        out_specs=(outside, outside, outside),
        scratch_shapes=[
            vmem((16, 4, OWN), bf16),
            vmem((2, 64), jnp.int32),
            vmem((1, 64), jnp.int32),
            vmem((8, 64), jnp.int32),
            vmem((4, 64), jnp.int32),
            vmem((8 * CHUNK, 256), bf16),
            vmem((8, 4, 16, OWN), bf16),
            vmem((16, 16, OWN), bf16),
            vmem((FEATS, 8 * CHUNK), bf16),
            vmem((rows, FEATS), bf16),
            vmem((rows, 256), f32),
            vmem((16, 2, OWN, 128), bf16),
            vmem((2, 16, OWN, 128), bf16),
            vmem((2, 3, OWN, 128), f32),
            vmem((2, 3, OWN, 128), f32),
            vmem((5, 64, LEAF), bf16),
            vmem((3, LEAF, LEAF), f32),
            vmem((2, 2, 16, 64), bf16),
            vmem((2, LEAF, 256), f32),
            vmem((2, LEAF, 256), f32),
            vmem((2, 64, 256), bf16),
            vmem((2, 64, 256), bf16),
            vmem((2, 64, LEAF), f32),
            vmem((3, 64, LEAF), f32),
            vmem((2, 64, 256), f32),
            dma((9,)), dma((16,)), dma((16,)), dma((4, 5)), dma((2, 5)), dma((2, 5)), dma((8, 5)), dma((2, 16)), dma((2, 16)), dma((2, 3)), dma((2, 3)),
            dma((2, 3)), dma((2, 3)), dma((5,)),
        ],
        compiler_params=pltpu.CompilerParams(collective_id=0, has_side_effects=True, vmem_limit_bytes=60 << 20),
    )(probes, points, leaf_skeleton, skeleton_one, skeleton_two, skeleton_three)
    leaf_interp, upper_interp, top_state = pl.pallas_call(
        finish_kernel, out_shape=outputs, in_specs=[inside] * 3, out_specs=(inside,) * 3)(*results)
    return leaf_interp.swapaxes(1, 2), upper_interp.swapaxes(1, 2)[:, None], top_state[:, None]


def solution(mesh):
    placed = (
        P(None, ("row", "col"), None),
        P(None, None, ("row", "col")),
        P(("row", "col"), None),
        P(("row", "col"), None),
        P("row", None),
        P("row", None),
    )
    return jax.shard_map(
        local,
        mesh=mesh,
        in_specs=placed,
        out_specs=(
            P(("row", "col"), None, None),
            P(None, ("row", "col"), None, None),
            P(None, ("row", "col"), None, None),
        ),
        check_vma=False,
    )
```

```python
import functools
import math

import jax
import jax.numpy as jnp
from jax import lax
from jax.experimental import pallas as pl
from jax.experimental.pallas import tpu as pltpu
from jax.sharding import PartitionSpec as P

LEAF = 128
MESH = pl.DeviceIdType.MESH
exact_mode = lax.Precision.HIGHEST
LOG2E = math.log2(math.e)
SIDE = 4
OWN = 256
CHUNK = 4 * OWN
FEATS = 64
PLACE = {(0, 0): 0, (0, 1): 1, (1, 0): 2, (3, 0): 3, (1, 1): 4, (3, 1): 5, (2, 0): 6, (2, 1): 7}
EARLY = 4
MIDWAY = 3


def pieces(value):
    high = value.astype(jnp.bfloat16).astype(jnp.float32)
    rest = value - high
    mid = rest.astype(jnp.bfloat16).astype(jnp.float32)
    return high, mid, rest - mid


def extra_rows(first, second, width=OWN):
    row = lax.broadcasted_iota(jnp.int32, (16, width), 0)
    out = jnp.zeros((16, width), jnp.float32)
    for i, value in enumerate((*first, *second)):
        out = jnp.where(row == i, value, out)
    return out


def exact(a, b, dims=((1,), (0,))):
    return lax.dot_general(a, b, (dims, ((), ())), precision=exact_mode, preferred_element_type=jnp.float32)

def split(v):
    h = v.astype(jnp.bfloat16)
    r = v - h.astype(jnp.float32)
    m = r.astype(jnp.bfloat16)
    return h, m, (r - m.astype(jnp.float32)).astype(jnp.bfloat16)

def select_rows(pick, values):
    return jnp.dot(jnp.concatenate([pick] * 3, axis=1), jnp.concatenate(split(values), axis=0), preferred_element_type=jnp.float32)

def pick_of(chosen):
    hits = lax.broadcasted_iota(jnp.int32, (128, 64), 0) == chosen
    return hits.astype(jnp.float32).T.astype(jnp.bfloat16)

def wide(col, width):
    return jnp.concatenate([col, col[:, :width - 128]], axis=1) if width > 128 else col[:, :width]

def eliminate(systems):
    width = systems[0].shape[1]
    sub = lax.broadcasted_iota(jnp.int32, (8, 1), 0)
    pivots = [m[0:8, :] for m in systems]
    systems = list(systems)
    for b in range(8):
        for s, m in enumerate(systems):
            p = pivots[s]
            lead = [jnp.broadcast_to(p[:, 8 * b + j:8 * b + j + 1], (8, 128)) for j in range(8)]
            for k in range(8):
                inv = 1.0 / lead[k][k:k + 1, :]
                f = lead[k] * inv
                q = p[k:k + 1, :]
                p = jnp.where(sub == k, q * wide(inv, width), p - wide(f, width) * q)
                for j in range(k + 1, 8):
                    q = lead[j][k:k + 1, :]
                    lead[j] = jnp.where(sub == k, q * inv, lead[j] - f * q)
            if b < 7:
                after = m[8 * b + 8:8 * b + 16, :]
                ahead = after
                for k in range(8):
                    ahead = ahead - wide(jnp.broadcast_to(after[:, 8 * b + k:8 * b + k + 1], (8, 128)), width) * p[k:k + 1, :]
                pivots[s] = ahead
            ch, cm, cl = split(m[:, 8 * b:8 * b + 8])
            ph, pm, low = split(p)
            change = jnp.dot(jnp.concatenate([ch, ch, cm, ch, cl, cm], axis=1), jnp.concatenate([ph, pm, ph, low, ph, pm], axis=0),
                             preferred_element_type=jnp.float32)
            rest = m - change
            systems[s] = jnp.concatenate(
                [p if i == b else pivots[s] if i == b + 1 else rest[8 * i:8 * i + 8, :] for i in range(8)], axis=0)
    return [m[:, 64:] for m in systems]


def interpolate(stacked, skeletons, picks):
    systems = []
    eye = lax.broadcasted_iota(jnp.int32, (64, 64), 0) == lax.broadcasted_iota(jnp.int32, (64, 64), 1)
    for y, z, pick in zip(stacked, skeletons, picks):
        cross = exact(z, y, ((1,), (1,)))
        gram = lax.dot_general(jnp.concatenate(split(cross), axis=1), jnp.concatenate([pick] * 3, axis=1), (((1,), (1,)), ((), ())), preferred_element_type=jnp.float32)
        diag = jnp.where(eye, gram, 0.0)
        ridge = jnp.sum(diag, keepdims=True) * (0.05 / 64) + 1e-5
        gram = gram + jnp.where(eye, ridge, 0.0)
        systems.append(jnp.concatenate([gram, cross], axis=1))
    return eliminate(systems)


def kernel_square(gain, feats):
    sq = jnp.sum(feats * feats, axis=0, keepdims=True)
    ones = (jnp.ones((1, 128), jnp.float32),) * 3
    left = jnp.concatenate([*pieces(feats * (LOG2E / 16)), extra_rows(pieces(math.log2(gain) - sq * (LOG2E / 32)), ones, 128)], axis=0)
    right = jnp.concatenate([feats, feats, feats, extra_rows(ones, pieces(sq * (-LOG2E / 32)), 128)], axis=0)
    power = jnp.dot(left.T.astype(jnp.bfloat16), right.astype(jnp.bfloat16), preferred_element_type=jnp.float32)
    child = lax.broadcasted_iota(jnp.int32, (128, 128), 0) // 64
    other = lax.broadcasted_iota(jnp.int32, (128, 128), 1) // 64
    return jnp.where(child == other, 0.0, jnp.exp2(power))


def hss_kernel(gain, probes, points, table_leaf, table_one, table_two, table_three, leaf_out, upper_out, top_out,
               raw, chosen_leaf, chosen_one, chosen_two, chosen_three, prb, pts, rpts, colf, rowf, acc, outbox, inbox, sum_out, sum_in, picks, square, pair_p, pair_z, pair_r, pair_out, pair_in, leaf_x, upper_x, top_x,
               loc_sem, rp_send, rp_recv, chip_send, up_send, down_send, got, box_send, box_recv, sum_send, sum_recv, pair_send, pair_recv, out_sem):
    tables = (table_leaf, table_one, table_two, table_three)
    row, col = lax.axis_index("row"), lax.axis_index("col")
    y, core = row // 2, lax.rem(row, 2)
    x, z = col // SIDE, lax.rem(col, SIDE)
    up = lax.rem(y + 1, SIDE) * 2 + core
    down = lax.rem(y + 3, SIDE) * 2 + core
    partner = y * 2 + 1 - core

    def shifted(dx, dz):
        return lax.rem(x + dx + SIDE, SIDE) * SIDE + lax.rem(z + dz + SIDE, SIDE)

    def far(i):
        return 1 + i, 1 + lax.rem(i // 3 + 1, 3), 1 + lax.rem(i + 1, 3)

    def line(k, half):
        d = 1 + lax.rem(k + 1, 3)
        return (10 + 2 * k, 0, d) if half == 0 else (11 + 2 * k, d, 0)

    barrier = pltpu.get_barrier_semaphore()
    for other in (up, down, partner):
        pl.semaphore_signal(barrier, inc=1, device_id=(other, col), device_id_type=MESH)

    def each_peer(action):
        def on_axis(k, _):
            for half in range(2):
                action(*line(k, half))
            return 0

        def off_axis(i, _):
            action(*far(i))
            return 0

        lax.fori_loop(0, 3, on_axis, 0)
        lax.fori_loop(0, 9, off_axis, 0)

    def greet(slot, dx, dz):
        pl.semaphore_signal(barrier, inc=1, device_id=(row, shifted(dx, dz)), device_id_type=MESH)

    each_peer(greet)
    local = [pltpu.make_async_copy(points, raw, loc_sem.at[4])]
    local += [pltpu.make_async_copy(probes.at[q], prb.at[pl.ds(q * OWN, OWN)], loc_sem.at[q]) for q in range(4)]
    for i, (src, dst) in enumerate(zip(tables, (chosen_leaf, chosen_one, chosen_two, chosen_three))):
        local.append(pltpu.make_async_copy(src, dst, loc_sem.at[5 + i]))
    for copy in local:
        copy.start()
    local[0].wait()
    feats = raw[...].astype(jnp.float32)
    for q in range(4):
        pts[0, q] = feats[:, q, :].astype(jnp.bfloat16)
    rpts[0] = pts[0, 0]
    for copy in local[1:]:
        copy.wait()

    bits = (lax.rem(col, 2), lax.rem(col // 2, 2))

    def pair_copy(level, kind):
        bit = bits[level]
        if kind == 2:
            src_ref, dst_ref = pair_out.at[level], pair_in.at[level]
        else:
            src_ref = pair_p.at[level, bit] if kind == 0 else pair_z.at[level, pl.ds(pl.multiple_of(bit * 64, 64), 64)]
            dst_ref = src_ref
        return pltpu.make_async_remote_copy(
            src_ref=src_ref, dst_ref=dst_ref, send_sem=pair_send.at[level, kind], recv_sem=pair_recv.at[level, kind],
            device_id=(row, col + (1 - 2 * bit) * (level + 1)), device_id_type=MESH)

    pl.semaphore_wait(barrier, 18)

    def row_copy(slot, dx, dz):
        return pltpu.make_async_remote_copy(
            src_ref=rpts.at[0], dst_ref=rpts.at[slot], send_sem=rp_send.at[slot], recv_sem=rp_recv.at[slot],
            device_id=(row, shifted(dx, dz)), device_id_type=MESH)

    def piece_copy(src, dst, q, sem, target):
        src_ref = pts.at[src] if q == 4 else prb.at[pl.ds(src * CHUNK + q * OWN, OWN)]
        dst_ref = pts.at[dst] if q == 4 else prb.at[pl.ds(dst * CHUNK + q * OWN, OWN)]
        return pltpu.make_async_remote_copy(
            src_ref=src_ref, dst_ref=dst_ref, send_sem=sem, recv_sem=got.at[dst, q],
            device_id=(target, col), device_id_type=MESH)

    def on_chip(dy, q):
        return piece_copy(PLACE[dy, 0], PLACE[dy, 1], q, chip_send.at[dy, q], partner)

    def upward(src_dy, q):
        return piece_copy(PLACE[src_dy, 0], PLACE[src_dy + 1, 0], q, up_send.at[src_dy, q], up)

    def downward(src_dy, q):
        return piece_copy(PLACE[src_dy, 0], PLACE[3 if src_dy == 0 else 2, 0], q, down_send.at[src_dy // 3, q], down)

    def arrived(dy, dc, q):
        place = PLACE[dy, dc]
        piece_copy(place, place, q, chip_send.at[0, 0], partner).wait_recv()

    on_chip(0, 4).start()
    upward(0, 4).start()
    downward(0, 4).start()
    each_peer(lambda slot, dx, dz: row_copy(slot, dx, dz).start())
    for q in range(4):
        on_chip(0, q).start()
    for q, r in zip((0, 1, 2, 3), (2, 3, 0, 1)):
        upward(0, q).start()
        downward(0, r).start()

    for leaf in range(2):
        picks[leaf] = pick_of(chosen_leaf[leaf:leaf + 1, :])
    picks[2] = pick_of(chosen_one[...])
    picks[3] = pick_of(chosen_two[pl.ds(col // 2, 1), :])
    picks[4] = pick_of(chosen_three[pl.ds(col // 4, 1), :])

    def picked(feats, pick):
        return lax.dot_general(feats, pick, (((1,), (1,)), ((), ())), preferred_element_type=jnp.float32)

    def child_points(level, feats):
        square[level] = kernel_square(gain, feats)
        if level < 2:
            pair_p[level, bits[level]] = picked(feats.astype(jnp.bfloat16), picks[2 + level]).astype(jnp.bfloat16)

    def pair_points(level):
        pair_copy(level, 0).wait_recv()
        return jnp.concatenate([pair_p[level, 0], pair_p[level, 1]], axis=1).astype(jnp.float32)

    child_points(0, jnp.concatenate([picked(pts[0, 0, :, leaf * LEAF:(leaf + 1) * LEAF], picks[leaf]) for leaf in range(2)], axis=1))
    pair_copy(0, 0).start()

    def col_features(place):
        for q in range(4):
            feats = pts[place, q].astype(jnp.float32)
            bias = jnp.sum(feats * feats, axis=0, keepdims=True) * (-LOG2E / 32)
            ones = (jnp.float32(1),) * 3
            stacked = jnp.concatenate([feats, feats, feats, extra_rows(ones, pieces(bias))], axis=0)
            colf[:, pl.ds(place * CHUNK + q * OWN, OWN)] = stacked.astype(jnp.bfloat16)

    def row_features(j):
        feats = rpts[j].astype(jnp.float32)
        bias = math.log2(gain) - jnp.sum(feats * feats, axis=0, keepdims=True) * (LOG2E / 32)
        ones = (jnp.float32(1),) * 3
        stacked = jnp.concatenate([*pieces(feats * (LOG2E / 16)), extra_rows(pieces(bias), ones)], axis=0)
        rowf[pl.ds(pl.multiple_of(j * OWN, OWN), OWN), :] = stacked.T.astype(jnp.bfloat16)

    def at(slot, count):
        return pl.ds(pl.multiple_of(slot * OWN, OWN), count * OWN)

    def partial(slot, count, first, last):
        cols = pl.ds(first * CHUNK, (last - first) * CHUNK)
        power = jnp.dot(rowf[at(slot, count), :], colf[:, cols], preferred_element_type=jnp.float32)
        return jnp.dot(jnp.exp2(power).astype(jnp.bfloat16), prb[cols, :], preferred_element_type=jnp.float32)

    col_features(0)
    row_features(0)
    power = jnp.dot(rowf[pl.ds(0, OWN), :], colf[:, pl.ds(0, CHUNK)], preferred_element_type=jnp.float32)
    leaf_of = lax.broadcasted_iota(jnp.int32, (OWN, CHUNK), 0) // LEAF
    other_leaf = lax.broadcasted_iota(jnp.int32, (OWN, CHUNK), 1) // LEAF
    tile = jnp.where(leaf_of == other_leaf, 0.0, jnp.exp2(power)).astype(jnp.bfloat16)
    own_sum = jnp.dot(tile, prb[pl.ds(0, CHUNK), :], preferred_element_type=jnp.float32)
    for q in (4, 0, 1, 2, 3):
        arrived(0, 1, q)
    col_features(1)
    acc[at(0, 1), :] = own_sum + partial(0, 1, 1, 2)

    def near_line(k, _):
        for half in range(2):
            slot, dx, dz = line(k, half)
            row_copy(slot, dx, dz).wait_recv()
            row_features(slot)
        acc[at(10 + 2 * k, 2), :] = partial(10 + 2 * k, 2, 0, 2)
        return 0

    def near_far(i, _):
        for e in range(3):
            slot, dx, dz = far(3 * i + e)
            row_copy(slot, dx, dz).wait_recv()
            row_features(slot)
        acc[at(1 + 3 * i, 3), :] = partial(1 + 3 * i, 3, 0, 2)
        return 0

    lax.fori_loop(0, 3, near_line, 0)
    for q in (4, 0, 1):
        arrived(1, 0, q)
        upward(1, q).start()
        on_chip(1, q).start()
    for q in (4, 2, 3):
        arrived(3, 0, q)
        if q != 4:
            downward(3, q).start()
        on_chip(3, q).start()
    lax.fori_loop(0, 3, near_far, 0)
    for q, r in ((2, 0), (3, 1)):
        arrived(1, 0, q)
        on_chip(1, q).start()
        arrived(3, 0, r)
        on_chip(3, r).start()
    for place in range(2, EARLY):
        col_features(place)
    child_points(1, pair_points(0))
    pair_copy(1, 0).start()

    def middle(i, _):
        @pl.when(i == MIDWAY)
        def _():
            for q in (4, 0, 2, 1, 3):
                arrived(2, 0, q)
                on_chip(2, q).start()

        acc[at(1 + 3 * i, 3), :] += partial(1 + 3 * i, 3, 2, EARLY)
        return 0

    lax.fori_loop(0, 5, middle, 0)
    child_points(2, pair_points(1))
    for dy in (1, 3, 2):
        for q in (4, 0, 1, 2, 3):
            arrived(dy, 1, q)
    for place in range(EARLY, 8):
        col_features(place)

    def box_copy(half, slot, dx, dz):
        target = shifted(-dx, 0) if half == 0 else shifted(0, -dz)
        return pltpu.make_async_remote_copy(
            src_ref=outbox.at[slot, half], dst_ref=inbox.at[half, slot],
            send_sem=box_send.at[half, slot], recv_sem=box_recv.at[half, slot],
            device_id=(row, target), device_id_type=MESH)

    def sum_copy(half, k):
        _, dx, dz = line(k, half)
        return pltpu.make_async_remote_copy(
            src_ref=sum_out.at[half, k], dst_ref=sum_in.at[half, k], send_sem=sum_send.at[half, k], recv_sem=sum_recv.at[half, k],
            device_id=(row, shifted(-dx, -dz)), device_id_type=MESH)

    def half_of(value, half):
        return value[:, half * 128:(half + 1) * 128]

    def far_blocks(i, _):
        total = acc[at(1 + 3 * i, 3), :] + partial(1 + 3 * i, 3, EARLY, 8)
        for e in range(3):
            slot, dx, dz = far(3 * i + e)
            for half in range(2):
                outbox[slot, half] = half_of(total[e * OWN:(e + 1) * OWN], half).astype(jnp.bfloat16)
                box_copy(half, slot, dx, dz).start()
        return 0

    def line_blocks(k, _):
        total = acc[at(10 + 2 * k, 2), :] + partial(10 + 2 * k, 2, EARLY, 8)
        for half in range(2):
            slot, dx, dz = line(k, half)
            mine, other = total[half * OWN:(half + 1) * OWN], 1 - half
            outbox[slot, other] = half_of(mine, other).astype(jnp.bfloat16)
            box_copy(other, slot, dx, dz).start()
            summed = half_of(mine, half)
            for e in range(3):
                source, dx, dz = far(3 * e + k if half == 0 else 3 * k + e)
                box_copy(half, source, dx, dz).wait_recv()
                summed = summed + inbox[half, source].astype(jnp.float32)
            sum_out[half, k] = summed
            sum_copy(half, k).start()
        return 0

    lax.fori_loop(0, 3, far_blocks, 0)
    lax.fori_loop(0, 3, line_blocks, 0)
    total = acc[at(0, 1), :] + partial(0, 1, 2, 8)
    for half in range(2):
        summed = half_of(total, half)
        for k in range(3):
            slot, dx, dz = line(k, 1 - half)
            box_copy(half, slot, dx, dz).wait_recv()
            summed = summed + inbox[half, slot].astype(jnp.float32)
            sum_copy(half, k).wait_recv()
            summed = summed + sum_in[half, k]
        acc[pl.ds(0, OWN), half * 128:(half + 1) * 128] = summed

    def leave(src, dst, sem):
        pltpu.make_async_copy(src, dst, sem).start()

    leaves = [acc[pl.ds(leaf * LEAF, LEAF), :] for leaf in range(2)]
    kept = [select_rows(picks[leaf], leaves[leaf]) for leaf in range(2)]
    solved = interpolate(leaves, kept, [picks[0], picks[1]])
    reduced = []
    for leaf, value in enumerate(solved):
        rows = prb[pl.ds(leaf * LEAF, LEAF), :]
        reduced.append(jnp.dot(jnp.concatenate(split(value), axis=1), jnp.concatenate([rows] * 3, axis=0), preferred_element_type=jnp.float32))
        leaf_x[leaf] = value
    leave(leaf_x, leaf_out, out_sem.at[0])
    below, weights = jnp.concatenate(kept, axis=0), jnp.concatenate(reduced, axis=0)
    for level in range(3):
        if level > 0:
            pair_copy(level - 1, 1).wait_recv()
            pair_copy(level - 1, 2).wait_recv()
            pair_r[level - 1, pl.ds(pl.multiple_of(64 - bits[level - 1] * 64, 64), 64), :] = pair_in[level - 1].astype(jnp.float32)
            below, weights = pair_z[level - 1], pair_r[level - 1]

        rows = below - exact(square[level], weights)
        skeleton = select_rows(picks[2 + level], rows)
        half = None if level == 2 else pl.ds(pl.multiple_of(bits[level] * 64, 64), 64)
        if level == 2:
            top_x[0] = skeleton
        else:
            pair_z[level, half, :] = skeleton
            pair_copy(level, 1).start()

        @pl.when(row >= 0)
        def _():
            (solved,) = interpolate([rows], [skeleton], [picks[2 + level]])
            value = exact(solved, weights)
            if level == 2:
                top_x[1] = value
                leave(top_x, top_out, out_sem.at[4])
            else:
                pair_out[level] = value.astype(jnp.bfloat16)
                pair_copy(level, 2).start()
                pair_r[level, half, :] = value
            upper_x[level] = solved
            leave(upper_x.at[level], upper_out.at[level], out_sem.at[1 + level])

    def drain(slot, dx, dz):
        row_copy(slot, dx, dz).wait_send()

    each_peer(drain)

    def drain_far(i, _):
        for half in range(2):
            box_copy(half, *far(i)).wait_send()
        return 0

    lax.fori_loop(0, 9, drain_far, 0)
    for k in range(3):
        for half in range(2):
            box_copy(half, *line(k, 1 - half)).wait_send()
            sum_copy(half, k).wait_send()
    for q in range(5):
        for dy in range(4):
            on_chip(dy, q).wait_send()
        upward(0, q).wait_send()
        downward(0, q).wait_send()
    for q in (4, 0, 1):
        upward(1, q).wait_send()
    for q in (2, 3):
        downward(3, q).wait_send()
    for level in range(2):
        for kind in range(3):
            pair_copy(level, kind).wait_send()
    pltpu.make_async_copy(leaf_x, leaf_out, out_sem.at[0]).wait()
    for level in range(3):
        pltpu.make_async_copy(upper_x.at[level], upper_out.at[level], out_sem.at[1 + level]).wait()
    pltpu.make_async_copy(top_x, top_out, out_sem.at[4]).wait()


def finish_kernel(leaf, upper, top, leaf_out, upper_out, top_out):
    leaf_out[...] = leaf[...]
    upper_out[...] = upper[...]
    top_out[...] = top[...]


def local(probes, points, leaf_skeleton, skeleton_one, skeleton_two, skeleton_three):
    bf16, f32, dma, vmem = jnp.bfloat16, jnp.float32, pltpu.SemaphoreType.DMA, pltpu.VMEM
    extent = OWN * lax.axis_size("row") * lax.axis_size("col")
    kernel_gain = 16.0 / math.sqrt(4 * extent)
    rows = 16 * OWN
    outside, inside = pl.BlockSpec(memory_space=pl.ANY), pl.BlockSpec(memory_space=vmem)
    outputs = (
        jax.ShapeDtypeStruct((2, 64, LEAF), f32),
        jax.ShapeDtypeStruct((3, 64, LEAF), f32),
        jax.ShapeDtypeStruct((2, 64, 256), f32),
    )
    results = pl.pallas_call(
        functools.partial(hss_kernel, kernel_gain),
        out_shape=outputs,
        in_specs=[outside] * 6,
        out_specs=(outside, outside, outside),
        scratch_shapes=[
            vmem((16, 4, OWN), bf16),
            vmem((2, 64), jnp.int32),
            vmem((1, 64), jnp.int32),
            vmem((8, 64), jnp.int32),
            vmem((4, 64), jnp.int32),
            vmem((8 * CHUNK, 256), bf16),
            vmem((8, 4, 16, OWN), bf16),
            vmem((16, 16, OWN), bf16),
            vmem((FEATS, 8 * CHUNK), bf16),
            vmem((rows, FEATS), bf16),
            vmem((rows, 256), f32),
            vmem((16, 2, OWN, 128), bf16),
            vmem((2, 16, OWN, 128), bf16),
            vmem((2, 3, OWN, 128), f32),
            vmem((2, 3, OWN, 128), f32),
            vmem((5, 64, LEAF), bf16),
            vmem((3, LEAF, LEAF), f32),
            vmem((2, 2, 16, 64), bf16),
            vmem((2, LEAF, 256), f32),
            vmem((2, LEAF, 256), f32),
            vmem((2, 64, 256), bf16),
            vmem((2, 64, 256), bf16),
            vmem((2, 64, LEAF), f32),
            vmem((3, 64, LEAF), f32),
            vmem((2, 64, 256), f32),
            dma((9,)), dma((16,)), dma((16,)), dma((4, 5)), dma((2, 5)), dma((2, 5)), dma((8, 5)), dma((2, 16)), dma((2, 16)), dma((2, 3)), dma((2, 3)),
            dma((2, 3)), dma((2, 3)), dma((5,)),
        ],
        compiler_params=pltpu.CompilerParams(collective_id=0, has_side_effects=True, vmem_limit_bytes=60 << 20),
    )(probes, points, leaf_skeleton, skeleton_one, skeleton_two, skeleton_three)
    leaf_interp, upper_interp, top_state = pl.pallas_call(
        finish_kernel, out_shape=outputs, in_specs=[inside] * 3, out_specs=(inside,) * 3)(*results)
    return leaf_interp.swapaxes(1, 2), upper_interp.swapaxes(1, 2)[:, None], top_state[:, None]


def solution(mesh):
    placed = (
        P(None, ("row", "col"), None),
        P(None, None, ("row", "col")),
        P(("row", "col"), None),
        P(("row", "col"), None),
        P("row", None),
        P("row", None),
    )
    return jax.shard_map(
        local,
        mesh=mesh,
        in_specs=placed,
        out_specs=(
            P(("row", "col"), None, None),
            P(None, ("row", "col"), None, None),
            P(None, ("row", "col"), None, None),
        ),
        check_vma=False,
    )
```

```python
import functools
import math

import jax
import jax.numpy as jnp
from jax import lax
from jax.experimental import pallas as pl
from jax.experimental.pallas import tpu as pltpu
from jax.sharding import PartitionSpec as P

LEAF = 128
MESH = pl.DeviceIdType.MESH
exact_mode = lax.Precision.HIGHEST
LOG2E = math.log2(math.e)
SIDE = 4
OWN = 256
CHUNK = 4 * OWN
FEATS = 64
PLACE = {(0, 0): 0, (0, 1): 1, (1, 0): 2, (3, 0): 3, (1, 1): 4, (3, 1): 5, (2, 0): 6, (2, 1): 7}
EARLY = 4
MIDWAY = 3


def pieces(value):
    high = value.astype(jnp.bfloat16).astype(jnp.float32)
    rest = value - high
    mid = rest.astype(jnp.bfloat16).astype(jnp.float32)
    return high, mid, rest - mid


def extra_rows(first, second, width=OWN):
    row = lax.broadcasted_iota(jnp.int32, (16, width), 0)
    out = jnp.zeros((16, width), jnp.float32)
    for i, value in enumerate((*first, *second)):
        out = jnp.where(row == i, value, out)
    return out


def exact(a, b, dims=((1,), (0,))):
    ah, am, _ = split(a)
    bh, bm, _ = split(b)
    left = jnp.concatenate([ah, ah, am], axis=1)
    right = jnp.concatenate([bh, bm, bh], axis=dims[1][0])
    return lax.dot_general(left, right, (dims, ((), ())), preferred_element_type=jnp.float32)


def split(v):
    h = v.astype(jnp.bfloat16)
    r = v - h.astype(jnp.float32)
    m = r.astype(jnp.bfloat16)
    return h, m, (r - m.astype(jnp.float32)).astype(jnp.bfloat16)

def select_rows(pick, values):
    return jnp.dot(jnp.concatenate([pick] * 3, axis=1), jnp.concatenate(split(values), axis=0), preferred_element_type=jnp.float32)

def pick_of(chosen):
    hits = lax.broadcasted_iota(jnp.int32, (128, 64), 0) == chosen
    return hits.astype(jnp.float32).T.astype(jnp.bfloat16)

def wide(col, width):
    return jnp.concatenate([col, col[:, :width - 128]], axis=1) if width > 128 else col[:, :width]

def eliminate(systems):
    width = systems[0].shape[1]
    sub = lax.broadcasted_iota(jnp.int32, (8, 1), 0)
    pivots = [m[0:8, :] for m in systems]
    systems = list(systems)
    for b in range(8):
        for s, m in enumerate(systems):
            p = pivots[s]
            lead = [jnp.broadcast_to(p[:, 8 * b + j:8 * b + j + 1], (8, 128)) for j in range(8)]
            for k in range(8):
                inv = 1.0 / lead[k][k:k + 1, :]
                f = lead[k] * inv
                q = p[k:k + 1, :]
                p = jnp.where(sub == k, q * wide(inv, width), p - wide(f, width) * q)
                for j in range(k + 1, 8):
                    q = lead[j][k:k + 1, :]
                    lead[j] = jnp.where(sub == k, q * inv, lead[j] - f * q)
            if b < 7:
                after = m[8 * b + 8:8 * b + 16, :]
                ahead = after
                for k in range(8):
                    ahead = ahead - wide(jnp.broadcast_to(after[:, 8 * b + k:8 * b + k + 1], (8, 128)), width) * p[k:k + 1, :]
                pivots[s] = ahead
            ch, cm, cl = split(m[:, 8 * b:8 * b + 8])
            ph, pm, low = split(p)
            change = jnp.dot(jnp.concatenate([ch, ch, cm, ch, cl, cm], axis=1), jnp.concatenate([ph, pm, ph, low, ph, pm], axis=0),
                             preferred_element_type=jnp.float32)
            rest = m - change
            systems[s] = jnp.concatenate(
                [p if i == b else pivots[s] if i == b + 1 else rest[8 * i:8 * i + 8, :] for i in range(8)], axis=0)
    return [m[:, 64:] for m in systems]


def interpolate(stacked, skeletons, picks):
    systems = []
    eye = lax.broadcasted_iota(jnp.int32, (64, 64), 0) == lax.broadcasted_iota(jnp.int32, (64, 64), 1)
    for y, z, pick in zip(stacked, skeletons, picks):
        cross = exact(z, y, ((1,), (1,)))
        gram = lax.dot_general(jnp.concatenate(split(cross), axis=1), jnp.concatenate([pick] * 3, axis=1), (((1,), (1,)), ((), ())), preferred_element_type=jnp.float32)
        diag = jnp.where(eye, gram, 0.0)
        ridge = jnp.sum(diag, keepdims=True) * (0.05 / 64) + 1e-5
        gram = gram + jnp.where(eye, ridge, 0.0)
        systems.append(jnp.concatenate([gram, cross], axis=1))
    return eliminate(systems)


def kernel_square(gain, feats):
    sq = jnp.sum(feats * feats, axis=0, keepdims=True)
    ones = (jnp.ones((1, 128), jnp.float32),) * 3
    left = jnp.concatenate([*pieces(feats * (LOG2E / 16)), extra_rows(pieces(math.log2(gain) - sq * (LOG2E / 32)), ones, 128)], axis=0)
    right = jnp.concatenate([feats, feats, feats, extra_rows(ones, pieces(sq * (-LOG2E / 32)), 128)], axis=0)
    power = jnp.dot(left.T.astype(jnp.bfloat16), right.astype(jnp.bfloat16), preferred_element_type=jnp.float32)
    child = lax.broadcasted_iota(jnp.int32, (128, 128), 0) // 64
    other = lax.broadcasted_iota(jnp.int32, (128, 128), 1) // 64
    return jnp.where(child == other, 0.0, jnp.exp2(power))


def hss_kernel(gain, probes, points, table_leaf, table_one, table_two, table_three, leaf_out, upper_out, top_out,
               raw, chosen_leaf, chosen_one, chosen_two, chosen_three, prb, pts, rpts, colf, rowf, acc, outbox, inbox, sum_out, sum_in, picks, square, pair_p, pair_z, pair_r, pair_out, pair_in, leaf_x, upper_x, top_x,
               loc_sem, rp_send, rp_recv, chip_send, up_send, down_send, got, box_send, box_recv, sum_send, sum_recv, pair_send, pair_recv, out_sem):
    tables = (table_leaf, table_one, table_two, table_three)
    row, col = lax.axis_index("row"), lax.axis_index("col")
    y, core = row // 2, lax.rem(row, 2)
    x, z = col // SIDE, lax.rem(col, SIDE)
    up = lax.rem(y + 1, SIDE) * 2 + core
    down = lax.rem(y + 3, SIDE) * 2 + core
    partner = y * 2 + 1 - core

    def shifted(dx, dz):
        return lax.rem(x + dx + SIDE, SIDE) * SIDE + lax.rem(z + dz + SIDE, SIDE)

    def far(i):
        return 1 + i, 1 + lax.rem(i // 3 + 1, 3), 1 + lax.rem(i + 1, 3)

    def line(k, half):
        d = 1 + lax.rem(k + 1, 3)
        return (10 + 2 * k, 0, d) if half == 0 else (11 + 2 * k, d, 0)

    barrier = pltpu.get_barrier_semaphore()
    for other in (up, down, partner):
        pl.semaphore_signal(barrier, inc=1, device_id=(other, col), device_id_type=MESH)

    def each_peer(action):
        def on_axis(k, _):
            for half in range(2):
                action(*line(k, half))
            return 0

        def off_axis(i, _):
            action(*far(i))
            return 0

        lax.fori_loop(0, 3, on_axis, 0)
        lax.fori_loop(0, 9, off_axis, 0)

    def greet(slot, dx, dz):
        pl.semaphore_signal(barrier, inc=1, device_id=(row, shifted(dx, dz)), device_id_type=MESH)

    each_peer(greet)
    local = [pltpu.make_async_copy(points, raw, loc_sem.at[4])]
    local += [pltpu.make_async_copy(probes.at[q], prb.at[pl.ds(q * OWN, OWN)], loc_sem.at[q]) for q in range(4)]
    for i, (src, dst) in enumerate(zip(tables, (chosen_leaf, chosen_one, chosen_two, chosen_three))):
        local.append(pltpu.make_async_copy(src, dst, loc_sem.at[5 + i]))
    for copy in local:
        copy.start()
    local[0].wait()
    feats = raw[...].astype(jnp.float32)
    for q in range(4):
        pts[0, q] = feats[:, q, :].astype(jnp.bfloat16)
    rpts[0] = pts[0, 0]
    for copy in local[1:]:
        copy.wait()

    bits = (lax.rem(col, 2), lax.rem(col // 2, 2))

    def pair_copy(level, kind):
        bit = bits[level]
        if kind == 2:
            src_ref, dst_ref = pair_out.at[level], pair_in.at[level]
        else:
            src_ref = pair_p.at[level, bit] if kind == 0 else pair_z.at[level, pl.ds(pl.multiple_of(bit * 64, 64), 64)]
            dst_ref = src_ref
        return pltpu.make_async_remote_copy(
            src_ref=src_ref, dst_ref=dst_ref, send_sem=pair_send.at[level, kind], recv_sem=pair_recv.at[level, kind],
            device_id=(row, col + (1 - 2 * bit) * (level + 1)), device_id_type=MESH)

    pl.semaphore_wait(barrier, 18)

    def row_copy(slot, dx, dz):
        return pltpu.make_async_remote_copy(
            src_ref=rpts.at[0], dst_ref=rpts.at[slot], send_sem=rp_send.at[slot], recv_sem=rp_recv.at[slot],
            device_id=(row, shifted(dx, dz)), device_id_type=MESH)

    def piece_copy(src, dst, q, sem, target):
        src_ref = pts.at[src] if q == 4 else prb.at[pl.ds(src * CHUNK + q * OWN, OWN)]
        dst_ref = pts.at[dst] if q == 4 else prb.at[pl.ds(dst * CHUNK + q * OWN, OWN)]
        return pltpu.make_async_remote_copy(
            src_ref=src_ref, dst_ref=dst_ref, send_sem=sem, recv_sem=got.at[dst, q],
            device_id=(target, col), device_id_type=MESH)

    def on_chip(dy, q):
        return piece_copy(PLACE[dy, 0], PLACE[dy, 1], q, chip_send.at[dy, q], partner)

    def upward(src_dy, q):
        return piece_copy(PLACE[src_dy, 0], PLACE[src_dy + 1, 0], q, up_send.at[src_dy, q], up)

    def downward(src_dy, q):
        return piece_copy(PLACE[src_dy, 0], PLACE[3 if src_dy == 0 else 2, 0], q, down_send.at[src_dy // 3, q], down)

    def arrived(dy, dc, q):
        place = PLACE[dy, dc]
        piece_copy(place, place, q, chip_send.at[0, 0], partner).wait_recv()

    on_chip(0, 4).start()
    upward(0, 4).start()
    downward(0, 4).start()
    each_peer(lambda slot, dx, dz: row_copy(slot, dx, dz).start())
    for q in range(4):
        on_chip(0, q).start()
    for q, r in zip((0, 1, 2, 3), (2, 3, 0, 1)):
        upward(0, q).start()
        downward(0, r).start()

    for leaf in range(2):
        picks[leaf] = pick_of(chosen_leaf[leaf:leaf + 1, :])
    picks[2] = pick_of(chosen_one[...])
    picks[3] = pick_of(chosen_two[pl.ds(col // 2, 1), :])
    picks[4] = pick_of(chosen_three[pl.ds(col // 4, 1), :])

    def picked(feats, pick):
        return lax.dot_general(feats, pick, (((1,), (1,)), ((), ())), preferred_element_type=jnp.float32)

    def child_points(level, feats):
        square[level] = kernel_square(gain, feats)
        if level < 2:
            pair_p[level, bits[level]] = picked(feats.astype(jnp.bfloat16), picks[2 + level]).astype(jnp.bfloat16)

    def pair_points(level):
        pair_copy(level, 0).wait_recv()
        return jnp.concatenate([pair_p[level, 0], pair_p[level, 1]], axis=1).astype(jnp.float32)

    child_points(0, jnp.concatenate([picked(pts[0, 0, :, leaf * LEAF:(leaf + 1) * LEAF], picks[leaf]) for leaf in range(2)], axis=1))
    pair_copy(0, 0).start()

    def col_features(place):
        for q in range(4):
            feats = pts[place, q].astype(jnp.float32)
            bias = jnp.sum(feats * feats, axis=0, keepdims=True) * (-LOG2E / 32)
            ones = (jnp.float32(1),) * 3
            stacked = jnp.concatenate([feats, feats, feats, extra_rows(ones, pieces(bias))], axis=0)
            colf[:, pl.ds(place * CHUNK + q * OWN, OWN)] = stacked.astype(jnp.bfloat16)

    def row_features(j):
        feats = rpts[j].astype(jnp.float32)
        bias = math.log2(gain) - jnp.sum(feats * feats, axis=0, keepdims=True) * (LOG2E / 32)
        ones = (jnp.float32(1),) * 3
        stacked = jnp.concatenate([*pieces(feats * (LOG2E / 16)), extra_rows(pieces(bias), ones)], axis=0)
        rowf[pl.ds(pl.multiple_of(j * OWN, OWN), OWN), :] = stacked.T.astype(jnp.bfloat16)

    def at(slot, count):
        return pl.ds(pl.multiple_of(slot * OWN, OWN), count * OWN)

    def partial(slot, count, first, last):
        cols = pl.ds(first * CHUNK, (last - first) * CHUNK)
        power = jnp.dot(rowf[at(slot, count), :], colf[:, cols], preferred_element_type=jnp.float32)
        return jnp.dot(jnp.exp2(power).astype(jnp.bfloat16), prb[cols, :], preferred_element_type=jnp.float32)

    col_features(0)
    row_features(0)
    power = jnp.dot(rowf[pl.ds(0, OWN), :], colf[:, pl.ds(0, CHUNK)], preferred_element_type=jnp.float32)
    leaf_of = lax.broadcasted_iota(jnp.int32, (OWN, CHUNK), 0) // LEAF
    other_leaf = lax.broadcasted_iota(jnp.int32, (OWN, CHUNK), 1) // LEAF
    tile = jnp.where(leaf_of == other_leaf, 0.0, jnp.exp2(power)).astype(jnp.bfloat16)
    own_sum = jnp.dot(tile, prb[pl.ds(0, CHUNK), :], preferred_element_type=jnp.float32)
    for q in (4, 0, 1, 2, 3):
        arrived(0, 1, q)
    col_features(1)
    acc[at(0, 1), :] = own_sum + partial(0, 1, 1, 2)

    def near_line(k, _):
        for half in range(2):
            slot, dx, dz = line(k, half)
            row_copy(slot, dx, dz).wait_recv()
            row_features(slot)
        acc[at(10 + 2 * k, 2), :] = partial(10 + 2 * k, 2, 0, 2)
        return 0

    def near_far(i, _):
        for e in range(3):
            slot, dx, dz = far(3 * i + e)
            row_copy(slot, dx, dz).wait_recv()
            row_features(slot)
        acc[at(1 + 3 * i, 3), :] = partial(1 + 3 * i, 3, 0, 2)
        return 0

    lax.fori_loop(0, 3, near_line, 0)
    for q in (4, 0, 1):
        arrived(1, 0, q)
        upward(1, q).start()
        on_chip(1, q).start()
    for q in (4, 2, 3):
        arrived(3, 0, q)
        if q != 4:
            downward(3, q).start()
        on_chip(3, q).start()
    lax.fori_loop(0, 3, near_far, 0)
    for q, r in ((2, 0), (3, 1)):
        arrived(1, 0, q)
        on_chip(1, q).start()
        arrived(3, 0, r)
        on_chip(3, r).start()
    for place in range(2, EARLY):
        col_features(place)
    child_points(1, pair_points(0))
    pair_copy(1, 0).start()

    def middle(i, _):
        @pl.when(i == MIDWAY)
        def _():
            for q in (4, 0, 2, 1, 3):
                arrived(2, 0, q)
                on_chip(2, q).start()

        acc[at(1 + 3 * i, 3), :] += partial(1 + 3 * i, 3, 2, EARLY)
        return 0

    lax.fori_loop(0, 5, middle, 0)
    child_points(2, pair_points(1))
    for dy in (1, 3, 2):
        for q in (4, 0, 1, 2, 3):
            arrived(dy, 1, q)
    for place in range(EARLY, 8):
        col_features(place)

    def box_copy(half, slot, dx, dz):
        target = shifted(-dx, 0) if half == 0 else shifted(0, -dz)
        return pltpu.make_async_remote_copy(
            src_ref=outbox.at[slot, half], dst_ref=inbox.at[half, slot],
            send_sem=box_send.at[half, slot], recv_sem=box_recv.at[half, slot],
            device_id=(row, target), device_id_type=MESH)

    def sum_copy(half, k):
        _, dx, dz = line(k, half)
        return pltpu.make_async_remote_copy(
            src_ref=sum_out.at[half, k], dst_ref=sum_in.at[half, k], send_sem=sum_send.at[half, k], recv_sem=sum_recv.at[half, k],
            device_id=(row, shifted(-dx, -dz)), device_id_type=MESH)

    def half_of(value, half):
        return value[:, half * 128:(half + 1) * 128]

    def far_blocks(i, _):
        total = acc[at(1 + 3 * i, 3), :] + partial(1 + 3 * i, 3, EARLY, 8)
        for e in range(3):
            slot, dx, dz = far(3 * i + e)
            for half in range(2):
                outbox[slot, half] = half_of(total[e * OWN:(e + 1) * OWN], half).astype(jnp.bfloat16)
                box_copy(half, slot, dx, dz).start()
        return 0

    def line_blocks(k, _):
        total = acc[at(10 + 2 * k, 2), :] + partial(10 + 2 * k, 2, EARLY, 8)
        for half in range(2):
            slot, dx, dz = line(k, half)
            mine, other = total[half * OWN:(half + 1) * OWN], 1 - half
            outbox[slot, other] = half_of(mine, other).astype(jnp.bfloat16)
            box_copy(other, slot, dx, dz).start()
            summed = half_of(mine, half)
            for e in range(3):
                source, dx, dz = far(3 * e + k if half == 0 else 3 * k + e)
                box_copy(half, source, dx, dz).wait_recv()
                summed = summed + inbox[half, source].astype(jnp.float32)
            sum_out[half, k] = summed
            sum_copy(half, k).start()
        return 0

    lax.fori_loop(0, 3, far_blocks, 0)
    lax.fori_loop(0, 3, line_blocks, 0)
    total = acc[at(0, 1), :] + partial(0, 1, 2, 8)
    for half in range(2):
        summed = half_of(total, half)
        for k in range(3):
            slot, dx, dz = line(k, 1 - half)
            box_copy(half, slot, dx, dz).wait_recv()
            summed = summed + inbox[half, slot].astype(jnp.float32)
            sum_copy(half, k).wait_recv()
            summed = summed + sum_in[half, k]
        acc[pl.ds(0, OWN), half * 128:(half + 1) * 128] = summed

    def leave(src, dst, sem):
        pltpu.make_async_copy(src, dst, sem).start()

    leaves = [acc[pl.ds(leaf * LEAF, LEAF), :] for leaf in range(2)]
    kept = [select_rows(picks[leaf], leaves[leaf]) for leaf in range(2)]
    solved = interpolate(leaves, kept, [picks[0], picks[1]])
    reduced = []
    for leaf, value in enumerate(solved):
        rows = prb[pl.ds(leaf * LEAF, LEAF), :]
        reduced.append(jnp.dot(jnp.concatenate(split(value), axis=1), jnp.concatenate([rows] * 3, axis=0), preferred_element_type=jnp.float32))
        leaf_x[leaf] = value
    leave(leaf_x, leaf_out, out_sem.at[0])
    below, weights = jnp.concatenate(kept, axis=0), jnp.concatenate(reduced, axis=0)
    for level in range(3):
        if level > 0:
            pair_copy(level - 1, 1).wait_recv()
            pair_copy(level - 1, 2).wait_recv()
            pair_r[level - 1, pl.ds(pl.multiple_of(64 - bits[level - 1] * 64, 64), 64), :] = pair_in[level - 1].astype(jnp.float32)
            below, weights = pair_z[level - 1], pair_r[level - 1]

        rows = below - exact(square[level], weights)
        skeleton = select_rows(picks[2 + level], rows)
        half = None if level == 2 else pl.ds(pl.multiple_of(bits[level] * 64, 64), 64)
        if level == 2:
            top_x[0] = skeleton
        else:
            pair_z[level, half, :] = skeleton
            pair_copy(level, 1).start()

        @pl.when(row >= 0)
        def _():
            (solved,) = interpolate([rows], [skeleton], [picks[2 + level]])
            value = exact(solved, weights)
            if level == 2:
                top_x[1] = value
                leave(top_x, top_out, out_sem.at[4])
            else:
                pair_out[level] = value.astype(jnp.bfloat16)
                pair_copy(level, 2).start()
                pair_r[level, half, :] = value
            upper_x[level] = solved
            leave(upper_x.at[level], upper_out.at[level], out_sem.at[1 + level])

    def drain(slot, dx, dz):
        row_copy(slot, dx, dz).wait_send()

    each_peer(drain)

    def drain_far(i, _):
        for half in range(2):
            box_copy(half, *far(i)).wait_send()
        return 0

    lax.fori_loop(0, 9, drain_far, 0)
    for k in range(3):
        for half in range(2):
            box_copy(half, *line(k, 1 - half)).wait_send()
            sum_copy(half, k).wait_send()
    for q in range(5):
        for dy in range(4):
            on_chip(dy, q).wait_send()
        upward(0, q).wait_send()
        downward(0, q).wait_send()
    for q in (4, 0, 1):
        upward(1, q).wait_send()
    for q in (2, 3):
        downward(3, q).wait_send()
    for level in range(2):
        for kind in range(3):
            pair_copy(level, kind).wait_send()
    pltpu.make_async_copy(leaf_x, leaf_out, out_sem.at[0]).wait()
    for level in range(3):
        pltpu.make_async_copy(upper_x.at[level], upper_out.at[level], out_sem.at[1 + level]).wait()
    pltpu.make_async_copy(top_x, top_out, out_sem.at[4]).wait()


def finish_kernel(leaf, upper, top, leaf_out, upper_out, top_out):
    leaf_out[...] = leaf[...]
    upper_out[...] = upper[...]
    top_out[...] = top[...]


def local(probes, points, leaf_skeleton, skeleton_one, skeleton_two, skeleton_three):
    bf16, f32, dma, vmem = jnp.bfloat16, jnp.float32, pltpu.SemaphoreType.DMA, pltpu.VMEM
    extent = OWN * lax.axis_size("row") * lax.axis_size("col")
    kernel_gain = 16.0 / math.sqrt(4 * extent)
    rows = 16 * OWN
    outside, inside = pl.BlockSpec(memory_space=pl.ANY), pl.BlockSpec(memory_space=vmem)
    outputs = (
        jax.ShapeDtypeStruct((2, 64, LEAF), f32),
        jax.ShapeDtypeStruct((3, 64, LEAF), f32),
        jax.ShapeDtypeStruct((2, 64, 256), f32),
    )
    results = pl.pallas_call(
        functools.partial(hss_kernel, kernel_gain),
        out_shape=outputs,
        in_specs=[outside] * 6,
        out_specs=(outside, outside, outside),
        scratch_shapes=[
            vmem((16, 4, OWN), bf16),
            vmem((2, 64), jnp.int32),
            vmem((1, 64), jnp.int32),
            vmem((8, 64), jnp.int32),
            vmem((4, 64), jnp.int32),
            vmem((8 * CHUNK, 256), bf16),
            vmem((8, 4, 16, OWN), bf16),
            vmem((16, 16, OWN), bf16),
            vmem((FEATS, 8 * CHUNK), bf16),
            vmem((rows, FEATS), bf16),
            vmem((rows, 256), f32),
            vmem((16, 2, OWN, 128), bf16),
            vmem((2, 16, OWN, 128), bf16),
            vmem((2, 3, OWN, 128), f32),
            vmem((2, 3, OWN, 128), f32),
            vmem((5, 64, LEAF), bf16),
            vmem((3, LEAF, LEAF), f32),
            vmem((2, 2, 16, 64), bf16),
            vmem((2, LEAF, 256), f32),
            vmem((2, LEAF, 256), f32),
            vmem((2, 64, 256), bf16),
            vmem((2, 64, 256), bf16),
            vmem((2, 64, LEAF), f32),
            vmem((3, 64, LEAF), f32),
            vmem((2, 64, 256), f32),
            dma((9,)), dma((16,)), dma((16,)), dma((4, 5)), dma((2, 5)), dma((2, 5)), dma((8, 5)), dma((2, 16)), dma((2, 16)), dma((2, 3)), dma((2, 3)),
            dma((2, 3)), dma((2, 3)), dma((5,)),
        ],
        compiler_params=pltpu.CompilerParams(collective_id=0, has_side_effects=True, vmem_limit_bytes=60 << 20),
    )(probes, points, leaf_skeleton, skeleton_one, skeleton_two, skeleton_three)
    leaf_interp, upper_interp, top_state = pl.pallas_call(
        finish_kernel, out_shape=outputs, in_specs=[inside] * 3, out_specs=(inside,) * 3)(*results)
    return leaf_interp.swapaxes(1, 2), upper_interp.swapaxes(1, 2)[:, None], top_state[:, None]


def solution(mesh):
    placed = (
        P(None, ("row", "col"), None),
        P(None, None, ("row", "col")),
        P(("row", "col"), None),
        P(("row", "col"), None),
        P("row", None),
        P("row", None),
    )
    return jax.shard_map(
        local,
        mesh=mesh,
        in_specs=placed,
        out_specs=(
            P(("row", "col"), None, None),
            P(None, ("row", "col"), None, None),
            P(None, ("row", "col"), None, None),
        ),
        check_vma=False,
    )
```
